128 devices in a mesh: gx: 4 (over z_lo, core), gy: 4 (over x), gz: 8 (over y, z_hi).
Axes of the slice: x: 4, y: 4, z: 4 (z_hi: 2, z_lo: 2; z = z_hi * 2 + z_lo), core: 2. Of those that a mesh axis runs over, the one named last changes fastest.
Arguments:
- features: bfloat16 [32, 32, 128, 96], P('gx', 'gy', 'gz'), may hold values from -10 to 10
- ground: int32 [32, 32], P('gx', 'gy'), may hold values from 0 to 64, as said below
- thickness: int32 [32, 32], P('gx', 'gy'), may hold values from 1 to 64
- weight_one: bfloat16 [27, 96, 96], replicated, may hold values from -0.125 to 0.125
- weight_two: bfloat16 [27, 96, 96], replicated, may hold values from -0.125 to 0.125
- gains: float32 [2, 96], replicated, may hold values from 0.5 to 1.5
- shifts: float32 [2, 96], replicated, may hold values from -3 to 3
- cotangent: bfloat16 [32, 32, 128, 96], P('gx', 'gy', 'gz'), may hold values from -6 to 6
Outputs:
- result: bfloat16 [32, 32, 128, 96], P('gx', 'gy', 'gz')
- grad_features: bfloat16 [32, 32, 128, 96], P('gx', 'gy', 'gz')
- grad_one: float32 [27, 96, 96], replicated
- grad_two: float32 [27, 96, 96], replicated
- norm_grads: float32 [4, 96], replicated
The draws below stay inside these ranges and needn't reach their ends.
Inputs may be any that keep to these rules, and one draw needn't show every extreme that they name: ground is constant over each aligned 8 x 8 footprint of vertical columns.
All inputs are finite; a program needn't handle non-finite values.
Results may differ from the reference program's by a relative error of at most 0.0058.
Values may be sent and summed in bfloat16 or wider, within the bound.
A program may use at most 128 MiB of HBM per device.

```python
import math
import jax
import jax.numpy as jnp
from jax import lax

C = 96
HX = 8
HY = 8
NX = 32
NY = 32
NZ = 128
THICK = 64


def draw_features(key, part):
    key_base = jax.random.fold_in(key, 101)
    key_offset = jax.random.fold_in(key, 102)
    offset = 0.6 * jax.random.normal(key_offset, (C,), jnp.float32)
    height = jnp.arange(NZ, dtype=jnp.float32) / NZ
    rising = jnp.power(3.0, height)
    base = jax.random.normal(key_base, (NX, NY, NZ, C), jnp.float32)
    values = (base + offset) * rising[None, None, :, None]
    return jnp.clip(values, -10.0, 10.0).astype(jnp.bfloat16)


def footprint(key):
    key_spot = jax.random.fold_in(key, 401)
    spot_x = jax.random.randint(jax.random.fold_in(key_spot, 1), (), 0, NX // HX, jnp.int32)
    spot_y = jax.random.randint(jax.random.fold_in(key_spot, 2), (), 0, NY // HY, jnp.int32)
    return (spot_x, spot_y)


def draw_ground(key, part):
    key_base = jax.random.fold_in(key, 201)
    spot_x, spot_y = footprint(key)
    grid_x = NX // HX
    top = NZ - THICK
    cols_x = NX // 8
    cols_y = NY // 8
    base = jax.random.randint(key_base, (cols_x, cols_y), 0, top + 1, jnp.int32)
    col_x = jnp.arange(cols_x, dtype=jnp.int32)
    col_y = jnp.arange(cols_y, dtype=jnp.int32)
    dev_x = col_x // (HX // 8)
    dev_y = col_y // (HY // 8)
    forced = (dev_x[:, None] == spot_x) & (dev_y[None, :] == spot_y)
    base = jnp.where(forced, 7, base)
    low_x = (spot_x + 1) % grid_x * (HX // 8)
    high_x = (spot_x + 2) % grid_x * (HX // 8)
    first_y = spot_y * (HY // 8)
    low = (col_x[:, None] == low_x) & (col_y[None, :] == first_y)
    high = (col_x[:, None] == high_x) & (col_y[None, :] == first_y)
    base = jnp.where(low, 0, base)
    base = jnp.where(high, top, base)
    return jnp.repeat(jnp.repeat(base, 8, axis=0), 8, axis=1)


def draw_thickness(key, part):
    key_thick = jax.random.fold_in(key, 301)
    spot_x, spot_y = footprint(key)
    grid_x = NX // HX
    values = jax.random.randint(key_thick, (NX, NY), 1, THICK + 1, jnp.int32)
    pos_x = jnp.arange(NX, dtype=jnp.int32)
    pos_y = jnp.arange(NY, dtype=jnp.int32)
    inside = ((pos_x // HX)[:, None] == spot_x) & ((pos_y // HY)[None, :] == spot_y)
    corner = ((pos_x % 8)[:, None] == 0) & ((pos_y % 8)[None, :] == 0)
    values = jnp.where(inside & corner, THICK, values)
    thin_x = (spot_x + 3) % grid_x * HX
    single = (pos_x[:, None] == thin_x) & (pos_y[None, :] == spot_y * HY)
    return jnp.where(single, 1, values)


def shard_levels(own_key, dims, split, low, largest):
    def one(axis_at, parts):
        heights = jax.random.uniform(jax.random.fold_in(jax.random.fold_in(own_key, 6), axis_at), (parts,), jnp.float32, low / len(split), largest / len(split))
        return jnp.repeat(jnp.exp(heights), dims[axis_at] // parts).reshape((-1,) + (1,) * (len(dims) - axis_at - 1))

    gain = one(*split[0])
    for cut in split[1:]:
        gain = gain * one(*cut)
    return gain


def scatter_about(rng, shape, spread, most, pieces=(), kind=jnp.bfloat16):
    factor_of = shard_levels(rng, shape, pieces, -0.22, 0.18) if pieces else 1.0
    entries = jax.random.normal(rng, shape, jnp.float32) * spread * factor_of
    return jnp.minimum(jnp.maximum(entries, -most), most).astype(kind)


def setup_inputs(seed: int = 0) -> dict:
    arg_keys = jax.random.split(jax.random.key(seed), 9)
    features = draw_features(jax.random.fold_in(arg_keys[8], 71), 0)
    ground = draw_ground(jax.random.fold_in(arg_keys[8], 71), 0)
    thickness = draw_thickness(jax.random.fold_in(arg_keys[8], 71), 0)
    weight_one = scatter_about(arg_keys[3], (27, C, C), (27 * C) ** -0.5, 0.125)
    weight_two = scatter_about(arg_keys[4], (27, C, C), (27 * C) ** -0.5, 0.125)
    gains = jnp.clip(jax.random.uniform(arg_keys[5], (2, C), jnp.float32, 0.5, 1.5), 0.5, 1.5)
    shifts = scatter_about(arg_keys[6], (2, C), 0.5, 3.0, (), jnp.float32)
    cotangent = scatter_about(arg_keys[7], (NX, NY, NZ, C), 1.0, 6.0, ((0, 4), (1, 4), (2, 8)))
    return dict(features=features, ground=ground, thickness=thickness, weight_one=weight_one, weight_two=weight_two, gains=gains, shifts=shifts, cotangent=cotangent)


def shifted(padded, start_x, start_y, start_z):
    return padded[start_x:start_x + NX, start_y:start_y + NY, start_z:start_z + NZ]

def convolve(values, weight, flipped):
    padded = jnp.pad(values.astype(jnp.float32), ((1, 1), (1, 1), (1, 1), (0, 0)))
    weight_f = weight.astype(jnp.float32)
    total = jnp.zeros((NX, NY, NZ, C), jnp.float32)
    for index in range(27):
        first, second, third = (index // 9, index // 3 % 3, index % 3)
        if flipped:
            window = shifted(padded, 2 - first, 2 - second, 2 - third)
            total = total + jnp.einsum('xyzo,io->xyzi', window, weight_f[index])
        else:
            window = shifted(padded, first, second, third)
            total = total + jnp.einsum('xyzi,io->xyzo', window, weight_f[index])
    return total

def weight_grad(values, grads):
    padded = jnp.pad(values.astype(jnp.float32), ((1, 1), (1, 1), (1, 1), (0, 0)))
    grads_f = grads.astype(jnp.float32)
    blocks = []
    for index in range(27):
        first, second, third = (index // 9, index // 3 % 3, index % 3)
        window = shifted(padded, first, second, third)
        blocks.append(jnp.einsum('xyzi,xyzo->io', window, grads_f))
    return jnp.stack(blocks)

def moments(values, mask_v, count):
    mean = lax.optimization_barrier(jnp.sum(values, axis=(0, 1, 2))) / count
    deviation = (values - mean) * mask_v
    var = lax.optimization_barrier(jnp.sum(deviation * deviation, axis=(0, 1, 2))) / count
    return (mean, lax.rsqrt(var + 1e-05))

def slope(pre):
    sig = jax.nn.sigmoid(pre)
    return sig * (1.0 + pre * (1.0 - sig))

def reference(features, ground, thickness, weight_one, weight_two, gains, shifts, cotangent):
    level = jnp.arange(NZ, dtype=jnp.int32)
    inside = (level[None, None, :] >= ground[:, :, None]) & (level[None, None, :] < (ground + thickness)[:, :, None])
    mask_f = inside.astype(jnp.float32)
    mask_v = mask_f[..., None]
    count = jnp.sum(mask_f)
    start = features * inside[..., None].astype(features.dtype)
    y_one = convolve(start, weight_one, False) * mask_v
    mean_one, rstd_one = moments(y_one, mask_v, count)
    norm_one = (y_one - mean_one) * rstd_one
    pre_one = gains[0] * norm_one + shifts[0]
    hidden = (jax.nn.silu(pre_one) * mask_v).astype(jnp.bfloat16)
    y_two = convolve(hidden, weight_two, False) * mask_v
    mean_two, rstd_two = moments(y_two, mask_v, count)
    norm_two = (y_two - mean_two) * rstd_two
    pre_two = gains[1] * norm_two + shifts[1] + start.astype(jnp.float32)
    result = (jax.nn.silu(pre_two) * mask_v).astype(jnp.bfloat16)
    d_two = cotangent.astype(jnp.float32) * mask_v * slope(pre_two)
    sum_two = lax.optimization_barrier(jnp.sum(d_two, axis=(0, 1, 2)))
    cross_two = lax.optimization_barrier(jnp.sum(d_two * norm_two, axis=(0, 1, 2)))
    dy_two = (mask_v * gains[1] * rstd_two * (d_two - sum_two / count - norm_two * cross_two / count)).astype(jnp.bfloat16)
    grad_w2 = weight_grad(hidden, dy_two)
    d_one = convolve(dy_two, weight_two, True) * mask_v * slope(pre_one)
    sum_one = lax.optimization_barrier(jnp.sum(d_one, axis=(0, 1, 2)))
    cross_one = lax.optimization_barrier(jnp.sum(d_one * norm_one, axis=(0, 1, 2)))
    dy_one = (mask_v * gains[0] * rstd_one * (d_one - sum_one / count - norm_one * cross_one / count)).astype(jnp.bfloat16)
    grad_w1 = weight_grad(start, dy_one)
    grad_features = (mask_v * (d_two + convolve(dy_one, weight_one, True))).astype(jnp.bfloat16)
    scale = 1.0 / math.sqrt(NX * NY * NZ / 8.0)
    norm_grads = jnp.stack([cross_one, sum_one, cross_two, sum_two]) * scale
    return (result, grad_features, grad_w1 * scale, grad_w2 * scale, norm_grads)
```

```python
import functools
import math

import jax
import jax.numpy as jnp
from jax import lax
from jax.experimental import pallas as pl
from jax.experimental.pallas import tpu as pltpu
from jax.sharding import PartitionSpec as P

MESH = pl.DeviceIdType.MESH
F32 = jnp.float32
BF16 = jnp.bfloat16
L = 128
SIDES = [(dx, dy) for dx in (-1, 0, 1) for dy in (-1, 0, 1) if (dx, dy) != (0, 0)]


def sigmoid(v):
    return 1.0 / (1.0 + jnp.exp(-v))


def body(
    dims,
    feat_ref, ground_ref, thick_ref, w1_ref, w2_ref, gains_ref, shifts_ref, cot_ref,
    result_ref, gfeat_ref, g1_ref, g2_ref, norm_ref,
    S, CT, Y1, Y2, D1, MK, N1, N2, D2,
    ZS, ZR, MZ, NZ1, NZ2, DZ2,
    V, PS, PH, PD2, PD1, DT, W1, W2, T1, T2, GS,
    STS, RX, RY, RZ,
    GA, GC, GB, GY, GD, GZ, GE, GX, GF,
    hs, hr, zs, zr, ss, sr, gs, gr,
):
    NGX, NGY, NGZ, X, Y, Z, C, seg = dims
    XE, YE = X + 2, Y + 2
    gx, gy, gz = lax.axis_index("gx"), lax.axis_index("gy"), lax.axis_index("gz")
    nz_lo, n_y = NGX // 2, NGZ // 2
    core, z_lo = gx % 2, gx // 2
    row_y, z_hi = gz // 2, gz % 2
    n_z = nz_lo * 2
    pos_z = z_hi * nz_lo + z_lo

    def dev(ax, ay, az):
        return (ax, ay, az)

    def peer_x(j):
        return dev((gx + j) % NGX, gy, gz)

    def peer_y(j):
        return dev(gx, (gy + j) % NGY, gz)

    def peer_z(j):
        return dev(gx, gy, (gz + j) % NGZ)

    def side(dx, dy):
        return dev((gx + dx + NGX) % NGX, (gy + dy + NGY) % NGY, gz)

    def grad_y(j):
        return dev(gx, gy, ((row_y + j) % n_y) * 2 + z_hi)

    def grad_z(j):
        other = (pos_z + j) % n_z
        return dev((other % nz_lo) * 2 + core, gy, row_y * 2 + other // nz_lo)

    partner = dev(z_lo * 2 + 1 - core, gy, gz)

    greet = [peer_x(j) for j in range(1, NGX)]
    greet += [peer_y(j) for j in range(1, NGY)]
    greet += [peer_z(j) for j in range(1, NGZ)]
    greet += [side(dx, dy) for dx, dy in SIDES if dx and dy]
    greet += [grad_z(j) for j in range(1, n_z)]
    barrier = pltpu.get_barrier_semaphore()
    for other in greet:
        pl.semaphore_signal(barrier, inc=1, device_id=other, device_id_type=MESH)

    for ref in (W1, W2, T1, T2, GS):
        ref[...] = jnp.zeros(ref.shape, ref.dtype)
    GS[0:2, 0:C] = gains_ref[...]
    GS[2:4, 0:C] = shifts_ref[...]

    def load_block(x, carry):
        level = lax.broadcasted_iota(jnp.int32, (Z, L), 0) + gz * Z
        for y in range(Y):
            low = ground_ref[x, y]
            high = low + thick_ref[x, y]
            m = jnp.where((level >= low) & (level < high), 1.0, 0.0).astype(F32)
            S[1 + x, 1 + y] = m
            S[1 + x, 1 + y, :, 0:C] = m[:, 0:C] * feat_ref[x, y].astype(F32)
            CT[1 + x, 1 + y] = jnp.zeros((Z, L), F32)
            CT[1 + x, 1 + y, :, 0:C] = cot_ref[x, y].astype(F32)
        return carry

    lax.fori_loop(0, X, load_block, 0)
    pl.semaphore_wait(barrier, len(greet))

    def cut(d, n, sending):
        if d == 0:
            return pl.ds(1, n)
        if sending:
            return pl.ds(n if d > 0 else 1, 1)
        return pl.ds(0 if d > 0 else n + 1, 1)

    def plane_copies(q, ref):
        out = []
        for k, (dx, dy) in enumerate(SIDES):
            out.append(
                pltpu.make_async_remote_copy(
                    src_ref=ref.at[cut(dx, X, True), cut(dy, Y, True)],
                    dst_ref=ref.at[cut(dx, X, False), cut(dy, Y, False)],
                    send_sem=hs.at[q, k],
                    recv_sem=hr.at[q, k],
                    device_id=side(dx, dy),
                    device_id_type=MESH,
                )
            )
        return out

    def face_copies(q):
        down = dev(gx, gy, (gz + NGZ - 1) % NGZ)
        up = dev(gx, gy, (gz + 1) % NGZ)
        out = []
        for k, other in ((0, down), (1, up)):
            out.append(
                pltpu.make_async_remote_copy(
                    src_ref=ZS.at[q, k],
                    dst_ref=ZR.at[q, 1 - k],
                    send_sem=zs.at[q, k],
                    recv_sem=zr.at[q, k],
                    device_id=other,
                    device_id_type=MESH,
                )
            )
        return out

    def start_all(copies):
        for c in copies:
            c.start()

    def wait_all(copies):
        for c in copies:
            c.wait()

    def send_faces(q, ref):
        def one(x, carry):
            ZS[q, 0, x] = ref[x, :, 0, :]
            ZS[q, 1, x] = ref[x, :, Z - 1, :]
            return carry

        lax.fori_loop(0, XE, one, 0)
        start_all(face_copies(q))

    def sum_copies(k, axis):
        n, me, peer, land = (
            (NGX, gx, peer_x, RX), (NGY, gy, peer_y, RY), (NGZ, gz, peer_z, RZ)
        )[axis]
        base = (0, NGX, NGX + NGY)[axis]
        out = []
        for j in range(1, n):
            out.append(
                pltpu.make_async_remote_copy(
                    src_ref=STS.at[k, axis],
                    dst_ref=land.at[k, me],
                    send_sem=ss.at[k, base + j],
                    recv_sem=sr.at[k, base + j],
                    device_id=peer(j),
                    device_id_type=MESH,
                )
            )
        return out

    def sum_start(k, axis, rows):
        at = lax.broadcasted_iota(jnp.int32, (8, L), 0)
        tile = jnp.zeros((8, L), F32)
        for i, row in enumerate(rows):
            tile = jnp.where(at == i, jnp.broadcast_to(row, (8, L)), tile)
        STS[k, axis] = tile
        me, land = ((gx, RX), (gy, RY), (gz, RZ))[axis]
        land[k, me] = tile
        start_all(sum_copies(k, axis))

    def sum_wait(k, axis, spread):
        n, land = ((NGX, RX), (NGY, RY), (NGZ, RZ))[axis]
        wait_all(sum_copies(k, axis))
        tiles = [land[k, i] for i in range(n)]
        rows = [[t[i : i + 1] for t in tiles] for i in range(3)]
        first = functools.reduce(jnp.add, rows[0])
        second = functools.reduce(jnp.add, rows[1])
        if not spread:
            return [first, second]
        count = functools.reduce(jnp.add, rows[2])
        mean = first / jnp.maximum(count, 1.0)
        for s, m in zip(rows[0], rows[2]):
            off = s / jnp.maximum(m, 1.0) - mean
            second = second + m * off * off
        return [first, second, count]

    def put(dest, x, main, low, high):
        V[:, 8 : 8 + Z, :] = main
        for y in range(YE):
            V[y, 7:8, :] = low[y : y + 1]
            V[y, 8 + Z : 9 + Z, :] = high[y : y + 1]
        for c in range(3):
            dest[x, :, :, c * L : (c + 1) * L] = V[:, 7 + c : 7 + c + Z, :].astype(BF16)

    H = X // 2

    def convolve(src, weights, flipped, finish):
        def half(h, carry):
            total = None
            for k0 in range(0, 9, 2):
                parts = []
                for k in range(k0, min(k0 + 2, 9)):
                    a, b = k // 3, k % 3
                    if flipped:
                        a, b = 2 - a, 2 - b
                    parts.append(
                        src[pl.ds(h * H + a, H), b : b + Y, :, :].reshape(H * Y * Z, 3 * L)
                    )
                left = jnp.concatenate(parts, axis=1) if len(parts) > 1 else parts[0]
                right = weights[k0 * 3 * L : (k0 * 3 + 3 * len(parts)) * L, :]
                term = jnp.dot(left, right, preferred_element_type=F32)
                total = term if total is None else total + term
            finish(h, total.reshape(H, Y, Z, L))
            return carry

        lax.fori_loop(0, 2, half, 0)

    def own(ref, h):
        return ref[pl.ds(1 + h * H, H), 1 : 1 + Y, :, :]

    def local_sum(terms):
        def one(x, carry):
            return tuple(c + jnp.sum(t, axis=0) for c, t in zip(carry, terms(1 + x)))

        zero = tuple(jnp.zeros((Z, L), F32) for _ in terms(1))
        out = lax.fori_loop(0, X, one, zero)
        return [jnp.sum(v, axis=0, keepdims=True) for v in out]

    def mid(ref, x):
        return ref[x, 1 : 1 + Y, :, :]

    def products(g, src, dy):
        flat = dy[1 : 1 + X, 1 : 1 + Y, :, L : 2 * L].reshape(X * Y * Z, L)
        DT[...] = flat.T

        def one(k, carry):
            a, b = k // 3, k % 3
            patch = src[pl.ds(a, X), pl.ds(b, Y), :, :].reshape(X * Y * Z, 3 * L)
            out = jnp.dot(DT[...], patch, preferred_element_type=F32)
            for c in range(3):
                GA[g, pl.ds(pl.multiple_of((3 * k + c) * C, 8), C), :] = (
                    out[:, c * L : (c + 1) * L].T[0:C]
                )
            return carry

        lax.fori_loop(0, 9, one, 0)

    len_z = seg
    len_y = seg * n_z
    len_c = seg * n_z * n_y
    chunk = seg

    def rows_at(off, n):
        return pl.ds(pl.multiple_of(off, 8), n)

    def grad_copies(g, stage):
        def copy(src, dst, k, other):
            return pltpu.make_async_remote_copy(
                src_ref=src, dst_ref=dst, send_sem=gs.at[g, stage, k],
                recv_sem=gr.at[g, stage, k], device_id=other, device_id_type=MESH,
            )

        off_c = core * len_c
        off_y = off_c + row_y * len_y
        off_z = off_y + pos_z * len_z
        out = []
        if stage == 0:
            out.append(copy(GA.at[g, rows_at((1 - core) * len_c, len_c)], GC.at[g], 0, partner))
        if stage == 1:
            for j in range(1, n_y):
                part = GB.at[g, rows_at(((row_y + j) % n_y) * len_y, len_y)]
                out.append(copy(part, GY.at[g, j - 1], j - 1, grad_y(j)))
        if stage == 2:
            for j in range(1, n_z):
                part = GD.at[g, rows_at(((pos_z + j) % n_z) * len_z, len_z)]
                out.append(copy(part, GZ.at[g, j - 1], j - 1, grad_z(j)))
        if stage == 3:
            for j in range(1, NGY):
                out.append(copy(GE.at[g], GX.at[g, gy], j - 1, peer_y(j)))
        if stage == 4:
            for j in range(1, n_z):
                part = GF.at[g, rows_at(off_z, len_z)]
                out.append(copy(part, part, j - 1, grad_z(j)))
        if stage == 5:
            for j in range(1, n_y):
                part = GF.at[g, rows_at(off_y, len_y)]
                out.append(copy(part, part, j - 1, grad_y(j)))
        if stage == 6:
            part = GF.at[g, rows_at(off_c, len_c)]
            out.append(copy(part, part, 0, partner))
        return out

    def grad_step(g, stage):
        if stage > 0:
            wait_all(grad_copies(g, stage - 1))
        if stage == 1:
            def fold(i, carry):
                at = rows_at(i * chunk, chunk)
                GB[g, at] = GA[g, rows_at(core * len_c + i * chunk, chunk)] + GC[g, at]
                return carry

            lax.fori_loop(0, len_c // chunk, fold, 0)
        if stage == 2:
            def fold(i, carry):
                at = rows_at(i * chunk, chunk)
                v = GB[g, rows_at(row_y * len_y + i * chunk, chunk)]
                for j in range(n_y - 1):
                    v = v + GY[g, j, at]
                GD[g, at] = v
                return carry

            lax.fori_loop(0, len_y // chunk, fold, 0)
        if stage == 3:
            v = GD[g, rows_at(pos_z * len_z, len_z)]
            for j in range(n_z - 1):
                v = v + GZ[g, j]
            GE[g] = v
            GX[g, gy] = v
        if stage == 4:
            v = GX[g, 0]
            for j in range(1, NGY):
                v = v + GX[g, j]
            GF[g, rows_at(core * len_c + row_y * len_y + pos_z * len_z, len_z)] = v
        if stage < 7:
            start_all(grad_copies(g, stage))

    total_cells = X * NGX * Y * NGY * Z * NGZ
    scale = 1.0 / math.sqrt(total_cells / 8.0)

    def grad_store(g, out_ref):
        def one(t, carry):
            out_ref[t] = GF[g, rows_at(t * C, C)][:, 0:C] * scale
            return carry

        lax.fori_loop(0, 27, one, 0)

    start_all(plane_copies(0, S))
    start_all(plane_copies(1, CT))

    def load_weights(t, carry):
        at = pl.ds(pl.multiple_of(t * L, L), C)
        whole = pl.ds(pl.multiple_of(t * L, L), L)
        W1[at, 0:C] = w1_ref[t]
        W2[at, 0:C] = w2_ref[t]
        back = pl.ds(pl.multiple_of((t - t % 3 + 2 - t % 3) * L, L), L)
        T1[back, :] = W1[whole, :].T
        T2[back, :] = W2[whole, :].T
        return carry

    lax.fori_loop(0, 27, load_weights, 0)

    wait_all(plane_copies(0, S))
    send_faces(0, S)
    wait_all(face_copies(0))

    at_y = lax.broadcasted_iota(jnp.int32, (YE, L), 0)
    live_y = jnp.where(
        ((at_y == 0) & (gy == 0)) | ((at_y == YE - 1) & (gy == NGY - 1)), 0.0, 1.0
    ).astype(F32)
    live_z = [jnp.where(gz == 0, 0.0, 1.0), jnp.where(gz == NGZ - 1, 0.0, 1.0)]

    def spread_lanes(v):
        return jnp.broadcast_to(v[..., L - 1 : L], v.shape)

    def first_input(x, carry):
        gone = ((x == 0) & (gx == 0)) | ((x == XE - 1) & (gx == NGX - 1))
        live = live_y * jnp.where(gone, 0.0, 1.0)
        s = S[x]
        m = spread_lanes(s) * live[:, None, :]
        MK[x] = m
        s = s * m
        S[x] = s
        faces = []
        for k in range(2):
            f = ZR[0, k, x]
            mf = spread_lanes(f) * (live * live_z[k])
            MZ[k, x] = mf
            f = f * mf
            ZR[0, k, x] = f
            faces.append(f)
        put(PS, x, s, faces[0], faces[1])
        return carry

    lax.fori_loop(0, XE, first_input, 0)

    def keep_y1(h, y):
        Y1[pl.ds(1 + h * H, H), 1 : 1 + Y, :, :] = y * own(MK, h)

    convolve(PS, W1, False, keep_y1)

    def norm_begin(k, ref):
        first, count = local_sum(lambda x: (mid(ref, x), mid(MK, x)))
        mean = first / jnp.maximum(count, 1.0)

        def deviation(x):
            d = (mid(ref, x) - mean) * mid(MK, x)
            return (d * d,)

        (second,) = local_sum(deviation)
        return [first, second, count]

    def norm_exchange(k, q, ref):
        rows = norm_begin(k, ref)
        sum_start(k, 0, rows)
        start_all(plane_copies(q, ref))
        rows = sum_wait(k, 0, True)
        sum_start(k, 1, rows)
        wait_all(plane_copies(q, ref))
        send_faces(q, ref)
        rows = sum_wait(k, 1, True)
        sum_start(k, 2, rows)
        wait_all(face_copies(q))
        rows = sum_wait(k, 2, True)
        mean = rows[0] / rows[2]
        rstd = lax.rsqrt(rows[1] / rows[2] + 1e-05)
        return mean, rstd, rows[2]

    mean1, rstd1, count = norm_exchange(0, 2, Y1)
    gain1, gain2, shift1, shift2 = GS[0:1], GS[1:2], GS[2:3], GS[3:4]

    def second_input(x, carry):
        def act(y, m):
            n = (y - mean1) * rstd1
            pre = gain1 * n + shift1
            return n, m * (pre * sigmoid(pre))

        n, hidden = act(Y1[x], MK[x])
        N1[x] = n
        faces = []
        for k in range(2):
            nf, hf = act(ZR[2, k, x], MZ[k, x])
            NZ1[k, x] = nf
            faces.append(hf)
        put(PH, x, hidden, faces[0], faces[1])
        return carry

    lax.fori_loop(0, XE, second_input, 0)

    def keep_y2(h, y):
        Y2[pl.ds(1 + h * H, H), 1 : 1 + Y, :, :] = y * own(MK, h)

    convolve(PH, W2, False, keep_y2)
    wait_all(plane_copies(1, CT))
    send_faces(1, CT)
    mean2, rstd2, _ = norm_exchange(1, 3, Y2)
    wait_all(face_copies(1))

    def outgoing(y, s, m, ct):
        n = (y - mean2) * rstd2
        pre = gain2 * n + shift2 + s
        sig = sigmoid(pre)
        return n, m * (pre * sig), ct * m * (sig * (1.0 + pre * (1.0 - sig)))

    lane = lax.broadcasted_iota(jnp.int32, (1, L), 1)
    inner = jnp.where(lane < C, 1.0, 0.0).astype(F32)

    def last_forward(x, carry):
        n, out, d = outgoing(Y2[x], S[x] * inner, MK[x], CT[x])
        N2[x] = n
        D2[x] = d

        @pl.when((x >= 1) & (x <= X))
        def _():
            result_ref[x - 1] = out[1 : 1 + Y, :, 0:C].astype(BF16)

        for k in range(2):
            nf, _, df = outgoing(ZR[3, k, x], ZR[0, k, x] * inner, MZ[k, x], ZR[1, k, x])
            NZ2[k, x] = nf
            DZ2[k, x] = df
        return carry

    lax.fori_loop(0, XE, last_forward, 0)

    rows = local_sum(lambda x: (mid(D2, x), mid(D2, x) * mid(N2, x)))
    for axis in range(3):
        sum_start(2, axis, rows)
        rows = sum_wait(2, axis, False)
    sum2, cross2 = rows

    def third_input(x, carry):
        factor = gain2 * rstd2

        def back(d, n, m):
            return m * factor * (d - sum2 / count - n * cross2 / count)

        main = back(D2[x], N2[x], MK[x])
        faces = [back(DZ2[k, x], NZ2[k, x], MZ[k, x]) for k in range(2)]
        put(PD2, x, main, faces[0], faces[1])
        return carry

    lax.fori_loop(0, XE, third_input, 0)

    def keep_d1(h, v):
        pre = gain1 * own(N1, h) + shift1
        sig = sigmoid(pre)
        D1[pl.ds(1 + h * H, H), 1 : 1 + Y, :, :] = (
            v * own(MK, h) * (sig * (1.0 + pre * (1.0 - sig)))
        )

    convolve(PD2, T2, True, keep_d1)
    rows = local_sum(lambda x: (mid(D1, x), mid(D1, x) * mid(N1, x)))
    sum_start(3, 0, rows)
    start_all(plane_copies(4, D1))
    products(1, PH, PD2)
    grad_step(1, 0)
    rows = sum_wait(3, 0, False)
    sum_start(3, 1, rows)
    wait_all(plane_copies(4, D1))
    send_faces(4, D1)
    rows = sum_wait(3, 1, False)
    sum_start(3, 2, rows)
    grad_step(1, 1)
    wait_all(face_copies(4))
    sum1, cross1 = sum_wait(3, 2, False)

    def fourth_input(x, carry):
        factor = gain1 * rstd1

        def back(d, n, m):
            return m * factor * (d - sum1 / count - n * cross1 / count)

        main = back(D1[x], N1[x], MK[x])
        faces = [back(ZR[4, k, x], NZ1[k, x], MZ[k, x]) for k in range(2)]
        put(PD1, x, main, faces[0], faces[1])
        return carry

    lax.fori_loop(0, XE, fourth_input, 0)
    products(0, PS, PD1)
    grad_step(0, 0)
    grad_step(1, 2)

    def keep_features(h, v):
        out = own(MK, h) * (own(D2, h) + v)
        gfeat_ref[pl.ds(h * H, H)] = out[:, :, :, 0:C].astype(BF16)

    convolve(PD1, T1, True, keep_features)
    at8 = lax.broadcasted_iota(jnp.int32, (8, L), 0)
    table = jnp.zeros((8, L), F32)
    for i, row in enumerate((cross1, sum1, cross2, sum2)):
        table = jnp.where(at8 == i, jnp.broadcast_to(row * scale, (8, L)), table)
    norm_ref[...] = table[0:4, 0:C]

    for stage in range(1, 8):
        grad_step(0, stage)
        if stage + 2 < 8:
            grad_step(1, stage + 2)
        if stage == 6:
            grad_store(1, g2_ref)
    grad_store(0, g1_ref)


def local(sizes, features, ground, thickness, weight_one, weight_two, gains, shifts, cotangent):
    NGX, NGY, NGZ = sizes
    X, Y, Z, C = features.shape
    n_y, n_z = NGZ // 2, NGX
    parts = 2 * n_y * n_z
    seg = -(-27 * C // (parts * 8)) * 8
    dims = (NGX, NGY, NGZ, X, Y, Z, C, seg)
    XE, YE = X + 2, Y + 2
    ext = pltpu.VMEM((XE, YE, Z, L), F32)
    face = pltpu.VMEM((2, XE, YE, L), F32)
    patch = pltpu.VMEM((XE, YE, Z, 3 * L), BF16)
    weights = pltpu.VMEM((27 * L, L), BF16)
    dma = pltpu.SemaphoreType.DMA
    scratch = [ext] * 9
    scratch += [pltpu.VMEM((5, 2, XE, YE, L), F32)] * 2
    scratch += [face] * 4
    scratch += [pltpu.VMEM((YE, Z + 16, L), F32)]
    scratch += [patch] * 4
    scratch += [pltpu.VMEM((L, X * Y * Z), BF16)]
    scratch += [weights] * 4
    scratch += [pltpu.VMEM((8, L), F32)]
    scratch += [pltpu.VMEM((4, 3, 8, L), F32)]
    scratch += [pltpu.VMEM((4, n, 8, L), F32) for n in (NGX, NGY, NGZ)]
    len_y, len_c = seg * n_z, seg * n_z * n_y
    scratch += [
        pltpu.VMEM((2, 2 * len_c, L), F32),
        pltpu.VMEM((2, len_c, L), F32),
        pltpu.VMEM((2, len_c, L), F32),
        pltpu.VMEM((2, max(n_y - 1, 1), len_y, L), F32),
        pltpu.VMEM((2, len_y, L), F32),
        pltpu.VMEM((2, n_z - 1, seg, L), F32),
        pltpu.VMEM((2, seg, L), F32),
        pltpu.VMEM((2, NGY, seg, L), F32),
        pltpu.VMEM((2, 2 * len_c, L), F32),
    ]
    sums = NGX + NGY + NGZ
    scratch += [dma((5, 8)), dma((5, 8)), dma((5, 2)), dma((5, 2))]
    scratch += [dma((4, sums)), dma((4, sums))]
    most = max(n_y, n_z, NGY) - 1
    scratch += [dma((2, 7, most)), dma((2, 7, most))]
    vmem = pl.BlockSpec(memory_space=pltpu.VMEM)
    smem = pl.BlockSpec(memory_space=pltpu.SMEM)
    return pl.pallas_call(
        functools.partial(body, dims),
        out_shape=(
            jax.ShapeDtypeStruct((X, Y, Z, C), BF16),
            jax.ShapeDtypeStruct((X, Y, Z, C), BF16),
            jax.ShapeDtypeStruct((27, C, C), F32),
            jax.ShapeDtypeStruct((27, C, C), F32),
            jax.ShapeDtypeStruct((4, C), F32),
        ),
        in_specs=[vmem, smem, smem, vmem, vmem, vmem, vmem, vmem],
        out_specs=(vmem,) * 5,
        scratch_shapes=scratch,
        compiler_params=pltpu.CompilerParams(
            collective_id=0, has_side_effects=True, vmem_limit_bytes=62 * 1024 * 1024
        ),
    )(features, ground, thickness, weight_one, weight_two, gains, shifts, cotangent)


def solution(mesh):
    sizes = tuple(mesh.shape[a] for a in ("gx", "gy", "gz"))
    return jax.shard_map(
        functools.partial(local, sizes),
        mesh=mesh,
        in_specs=(
            P("gx", "gy", "gz", None),
            P("gx", "gy"),
            P("gx", "gy"),
            P(),
            P(),
            P(),
            P(),
            P("gx", "gy", "gz", None),
        ),
        out_specs=(P("gx", "gy", "gz", None), P("gx", "gy", "gz", None), P(), P(), P()),
        check_vma=False,
    )
```

```python
import functools
import math

import jax
import jax.numpy as jnp
from jax import lax
from jax.experimental import pallas as pl
from jax.experimental.pallas import tpu as pltpu
from jax.sharding import PartitionSpec as P

MESH = pl.DeviceIdType.MESH
F32 = jnp.float32
BF16 = jnp.bfloat16
L = 128
SIDES = [(dx, dy) for dx in (-1, 0, 1) for dy in (-1, 0, 1) if (dx, dy) != (0, 0)]


def sigmoid(v):
    return 1.0 / (1.0 + jnp.exp(-v))


def body(
    dims,
    feat_in, ground_in, thick_in, w1_in, w2_in, gains_in, shifts_in, cot_in,
    result_out, gfeat_out, g1_out, g2_out, norm_out,
    feat_ref, cot_ref, w1_ref, w2_ref, gains_ref, shifts_ref, ground_ref, thick_ref,
    result_ref, gfeat_ref, g1_ref, g2_ref, norm_ref,
    S, CT, Y1, Y2, D1, MK, N1, N2, D2,
    ZS, ZR, MZ, NZ1, NZ2, DZ2,
    V, PS, PH, PD2, PD1, DT, W1, W2, T1, T2, GS,
    STS, RA, RB,
    GA, GC, GF, *rest,
):
    NGX, NGY, NGZ, X, Y, Z, C, segs = dims
    portions = [rest[6 * p : 6 * p + 6] for p in range(3)]
    hs, hr, zs, zr, ss, sr, gs, gr, ins, outs = rest[18:]
    XE, YE = X + 2, Y + 2
    gx, gy, gz = lax.axis_index("gx"), lax.axis_index("gy"), lax.axis_index("gz")
    nz_lo, n_y = NGX // 2, NGZ // 2
    core, z_lo = gx % 2, gx // 2
    row_y, z_hi = gz // 2, gz % 2
    n_z = nz_lo * 2
    pos_z = z_hi * nz_lo + z_lo

    def dev(ax, ay, az):
        return (ax, ay, az)

    def peer_y(j):
        return dev(gx, (gy + j) % NGY, gz)

    def side(dx, dy):
        return dev((gx + dx + NGX) % NGX, (gy + dy + NGY) % NGY, gz)

    def grad_y(j):
        return dev(gx, gy, ((row_y + j) % n_y) * 2 + z_hi)

    def grad_z(j):
        other = (pos_z + j) % n_z
        return dev((other % nz_lo) * 2 + core, gy, row_y * 2 + other // nz_lo)

    partner = dev(z_lo * 2 + 1 - core, gy, gz)
    n_a, n_b = 2 * n_z, NGY * n_y
    me_a, me_b = pos_z * 2 + core, gy * n_y + row_y

    def peer_a(j):
        other = (me_a + j) % n_a
        pos = other // 2
        return dev((pos % nz_lo) * 2 + other % 2, gy, row_y * 2 + pos // nz_lo)

    def peer_b(j):
        other = (me_b + j) % n_b
        return dev(gx, other // n_y, (other % n_y) * 2 + z_hi)

    down = dev(gx, gy, (gz + NGZ - 1) % NGZ)
    up = dev(gx, gy, (gz + 1) % NGZ)

    greet = [peer_a(j) for j in range(1, n_a)]
    greet += [peer_b(j) for j in range(1, n_b)]
    greet += [down, up]
    greet += [side(dx, dy) for dx, dy in SIDES]
    barrier = pltpu.get_barrier_semaphore()
    for other in greet:
        pl.semaphore_signal(barrier, inc=1, device_id=other, device_id_type=MESH)

    arrivals = [
        pltpu.make_async_copy(src, dst, ins.at[i])
        for i, (src, dst) in enumerate(
            (
                (ground_in, ground_ref), (thick_in, thick_ref), (feat_in, feat_ref),
                (cot_in, cot_ref), (w1_in, w1_ref), (gains_in, gains_ref),
                (shifts_in, shifts_ref), (w2_in, w2_ref),
            )
        )
    ]
    for c in arrivals:
        c.start()

    for ref in (W1, W2, T1, T2, GS):
        ref[...] = jnp.zeros(ref.shape, ref.dtype)
    for c in arrivals[:4]:
        c.wait()

    def load_block(x, carry):
        level = lax.broadcasted_iota(jnp.int32, (Z, L), 0) + gz * Z
        for y in range(Y):
            low = ground_ref[x, y]
            high = low + thick_ref[x, y]
            m = jnp.where((level >= low) & (level < high), 1.0, 0.0).astype(F32)
            S[1 + x, 1 + y] = m
            S[1 + x, 1 + y, :, 0:C] = m[:, 0:C] * feat_ref[x, y].astype(F32)
            CT[1 + x, 1 + y] = jnp.zeros((Z, L), F32)
            CT[1 + x, 1 + y, :, 0:C] = cot_ref[x, y].astype(F32)
        return carry

    lax.fori_loop(0, X, load_block, 0)
    pl.semaphore_wait(barrier, len(greet))

    def cut(d, n, sending):
        if d == 0:
            return pl.ds(1, n)
        if sending:
            return pl.ds(n if d > 0 else 1, 1)
        return pl.ds(0 if d > 0 else n + 1, 1)

    def plane_copies(q, ref):
        out = []
        for k, (dx, dy) in enumerate(SIDES):
            out.append(
                pltpu.make_async_remote_copy(
                    src_ref=ref.at[cut(dx, X, True), cut(dy, Y, True)],
                    dst_ref=ref.at[cut(dx, X, False), cut(dy, Y, False)],
                    send_sem=hs.at[q, k],
                    recv_sem=hr.at[q, k],
                    device_id=side(dx, dy),
                    device_id_type=MESH,
                )
            )
        return out

    def face_copies(q):
        out = []
        for k, other in ((0, down), (1, up)):
            out.append(
                pltpu.make_async_remote_copy(
                    src_ref=ZS.at[q, k],
                    dst_ref=ZR.at[q, 1 - k],
                    send_sem=zs.at[q, k],
                    recv_sem=zr.at[q, k],
                    device_id=other,
                    device_id_type=MESH,
                )
            )
        return out

    def start_all(copies):
        for c in copies:
            c.start()

    def wait_all(copies):
        for c in copies:
            c.wait()

    def send_faces(q, ref):
        def one(x, carry):
            ZS[q, 0, x] = ref[x, :, 0, :]
            ZS[q, 1, x] = ref[x, :, Z - 1, :]
            return carry

        lax.fori_loop(0, XE, one, 0)
        start_all(face_copies(q))

    def sum_copies(k, part):
        n, me, peer, land = ((n_a, me_a, peer_a, RA), (n_b, me_b, peer_b, RB))[part]
        base = (0, n_a)[part]
        return [
            pltpu.make_async_remote_copy(
                src_ref=STS.at[k, part],
                dst_ref=land.at[k, me],
                send_sem=ss.at[base + j],
                recv_sem=sr.at[k, base + j],
                device_id=peer(j),
                device_id_type=MESH,
            )
            for j in range(1, n)
        ]

    def sum_start(k, part, rows):
        at = lax.broadcasted_iota(jnp.int32, (4, L), 0)
        tile = jnp.zeros((4, L), F32)
        for i, row in enumerate(rows):
            tile = jnp.where(at == i, jnp.broadcast_to(row, (4, L)), tile)
        STS[k, part] = tile
        me, land = ((me_a, RA), (me_b, RB))[part]
        land[k, me] = tile
        start_all(sum_copies(k, part))

    def sum_wait(k, part, spread):
        n, land = ((n_a, RA), (n_b, RB))[part]
        wait_all(sum_copies(k, part))
        tiles = land[k]
        first, second, third = (jnp.sum(tiles[:, i], axis=0, keepdims=True) for i in range(3))
        if not spread:
            return [first, second]
        mean = first / jnp.maximum(third, 1.0)
        each = tiles[:, 0] / jnp.maximum(tiles[:, 2], 1.0) - mean
        second = second + jnp.sum(tiles[:, 2] * each * each, axis=0, keepdims=True)
        return [first, second, third]

    def put(dest, x, main, low, high):
        V[:, 8 : 8 + Z, :] = main
        for y in range(YE):
            V[y, 7:8, :] = low[y : y + 1]
            V[y, 8 + Z : 9 + Z, :] = high[y : y + 1]
        for c in range(3):
            dest[x, :, :, c * L : (c + 1) * L] = V[:, 7 + c : 7 + c + Z, :].astype(BF16)

    H = X // 2

    def convolve(src, weights, flipped, finish):
        def half(h, carry):
            total = None
            for k0 in range(0, 9, 2):
                parts = []
                for k in range(k0, min(k0 + 2, 9)):
                    a, b = k // 3, k % 3
                    if flipped:
                        a, b = 2 - a, 2 - b
                    parts.append(
                        src[pl.ds(h * H + a, H), b : b + Y, :, :].reshape(H * Y * Z, 3 * L)
                    )
                left = jnp.concatenate(parts, axis=1) if len(parts) > 1 else parts[0]
                right = weights[k0 * 3 * L : (k0 * 3 + 3 * len(parts)) * L, :]
                term = jnp.dot(left, right, preferred_element_type=F32)
                total = term if total is None else total + term
            finish(h, total.reshape(H, Y, Z, L))
            return carry

        lax.fori_loop(0, 2, half, 0)

    def own(ref, h):
        return ref[pl.ds(1 + h * H, H), 1 : 1 + Y, :, :]

    def local_sum(terms):
        def one(x, carry):
            return tuple(c + jnp.sum(t, axis=0) for c, t in zip(carry, terms(1 + x)))

        zero = tuple(jnp.zeros((Z, L), F32) for _ in terms(1))
        out = lax.fori_loop(0, X, one, zero)
        return [jnp.sum(v, axis=0, keepdims=True) for v in out]

    def mid(ref, x):
        return ref[x, 1 : 1 + Y, :, :]

    def prepare(dy):
        flat = dy[1 : 1 + X, 1 : 1 + Y, :, L : 2 * L].reshape(X * Y * Z, L)
        DT[...] = flat.T

    def products(g, src, first, last):
        def one(k, carry):
            a, b = k // 3, k % 3
            patch = src[pl.ds(a, X), pl.ds(b, Y), :, :].reshape(X * Y * Z, 3 * L)
            out = jnp.dot(DT[...], patch, preferred_element_type=F32)
            for c in range(3):
                GA[g, pl.ds(pl.multiple_of((3 * k + c) * C, 8), C), :] = (
                    out[:, c * L : (c + 1) * L].T[0:C]
                )
            return carry

        lax.fori_loop(first, last, one, 0)

    axes = ((n_y, row_y, grad_y), (n_z, pos_z, grad_z), (NGY, gy, peer_y))
    plans = []
    base = 0
    for p in range(3):
        plan = [axes[(p + i) % 3] for i in range(3)]
        len1 = plan[1][0] * segs[p]
        plans.append((plan, base, len1, segs[p]))
        base += plan[0][0] * len1
    len_c = base

    def rows_at(off, n):
        return pl.ds(pl.multiple_of(off, 8), n)

    most = max(n_y, n_z, NGY) - 1

    def grad_copies(g, stage):
        def copy(src, dst, k, other):
            return pltpu.make_async_remote_copy(
                src_ref=src, dst_ref=dst, send_sem=gs.at[g, stage, k],
                recv_sem=gr.at[g, stage, k], device_id=other, device_id_type=MESH,
            )

        if stage == 0:
            return [copy(GA.at[g, rows_at((1 - core) * len_c, len_c)], GC.at[g], 0, partner)]
        if stage == 6:
            part = GF.at[g, rows_at(core * len_c, len_c)]
            return [copy(part, part, 0, partner)]
        out = []
        for p, (plan, base, len1, seg) in enumerate(plans):
            GB, GY, GD, GZ, GE, GX = portions[p]
            n, me, peer = plan[(None, 0, 1, 2, 1, 0)[stage]]
            off1 = core * len_c + base + plan[0][1] * len1
            off2 = off1 + plan[1][1] * seg
            for j in range(1, n):
                if stage == 1:
                    part = GB.at[g, rows_at(((me + j) % n) * len1, len1)]
                    land = GY.at[g, j - 1]
                elif stage == 2:
                    part = GD.at[g, rows_at(((me + j) % n) * seg, seg)]
                    land = GZ.at[g, j - 1]
                elif stage == 3:
                    part, land = GE.at[g], GX.at[g, me]
                elif stage == 4:
                    part = land = GF.at[g, rows_at(off2, seg)]
                else:
                    part = land = GF.at[g, rows_at(off1, len1)]
                out.append(copy(part, land, p * most + j - 1, peer(j)))
        return out

    def grad_step(g, stage):
        if stage > 0:
            wait_all(grad_copies(g, stage - 1))
        for p, (plan, base, len1, seg) in enumerate(plans):
            GB, GY, GD, GZ, GE, GX = portions[p]
            if stage == 1:
                def fold(i, carry):
                    at = i * len1 + base
                    GB[g, rows_at(i * len1, len1)] = (
                        GA[g, rows_at(core * len_c + at, len1)] + GC[g, rows_at(at, len1)]
                    )
                    return carry

                lax.fori_loop(0, plan[0][0], fold, 0)
            if stage == 2:
                v = GB[g, rows_at(plan[0][1] * len1, len1)]
                for j in range(plan[0][0] - 1):
                    v = v + GY[g, j]
                GD[g] = v
            if stage == 3:
                v = GD[g, rows_at(plan[1][1] * seg, seg)]
                for j in range(plan[1][0] - 1):
                    v = v + GZ[g, j]
                GE[g] = v
                GX[g, plan[2][1]] = v
            if stage == 4:
                v = GX[g, 0]
                for j in range(1, plan[2][0]):
                    v = v + GX[g, j]
                off = core * len_c + base + plan[0][1] * len1 + plan[1][1] * seg
                GF[g, rows_at(off, seg)] = v
        if stage < 7:
            start_all(grad_copies(g, stage))

    total_cells = X * NGX * Y * NGY * Z * NGZ
    scale = 1.0 / math.sqrt(total_cells / 8.0)

    def grad_store(g, out_ref):
        def one(t, carry):
            out_ref[t] = GF[g, rows_at(t * C, C)][:, 0:C] * scale
            return carry

        lax.fori_loop(0, 27, one, 0)

    start_all(plane_copies(0, S))
    for c in arrivals[4:7]:
        c.wait()
    GS[0:2, 0:C] = gains_ref[...]
    GS[2:4, 0:C] = shifts_ref[...]

    def load_first(t, carry):
        W1[pl.ds(pl.multiple_of(t * L, L), C), 0:C] = w1_ref[t]
        return carry

    lax.fori_loop(0, 27, load_first, 0)

    def load_rest(t, carry):
        W2[pl.ds(pl.multiple_of(t * L, L), C), 0:C] = w2_ref[t]
        whole = pl.ds(pl.multiple_of(t * L, L), L)
        back = pl.ds(pl.multiple_of((t - t % 3 + 2 - t % 3) * L, L), L)
        T1[back, :] = W1[whole, :].T
        T2[back, :] = W2[whole, :].T
        return carry

    def fill_weights():
        arrivals[7].wait()
        lax.fori_loop(0, 27, load_rest, 0)

    wait_all(plane_copies(0, S))
    send_faces(0, S)
    wait_all(face_copies(0))
    start_all(plane_copies(1, CT))

    at_y = lax.broadcasted_iota(jnp.int32, (YE, L), 0)
    live_y = jnp.where(
        ((at_y == 0) & (gy == 0)) | ((at_y == YE - 1) & (gy == NGY - 1)), 0.0, 1.0
    ).astype(F32)
    live_z = [jnp.where(gz == 0, 0.0, 1.0), jnp.where(gz == NGZ - 1, 0.0, 1.0)]

    def spread_lanes(v):
        return jnp.broadcast_to(v[..., L - 1 : L], v.shape)

    def first_input(x, carry):
        gone = ((x == 0) & (gx == 0)) | ((x == XE - 1) & (gx == NGX - 1))
        live = live_y * jnp.where(gone, 0.0, 1.0)
        s = S[x]
        m = spread_lanes(s) * live[:, None, :]
        MK[x] = m
        s = s * m
        S[x] = s
        faces = []
        for k in range(2):
            f = ZR[0, k, x]
            mf = spread_lanes(f) * (live * live_z[k])
            MZ[k, x] = mf
            f = f * mf
            ZR[0, k, x] = f
            faces.append(f)
        put(PS, x, s, faces[0], faces[1])
        return carry

    lax.fori_loop(0, XE, first_input, 0)

    def keep_y1(h, y):
        Y1[pl.ds(1 + h * H, H), 1 : 1 + Y, :, :] = y * own(MK, h)

    convolve(PS, W1, False, keep_y1)

    def norm_begin(k, ref):
        first, count = local_sum(lambda x: (mid(ref, x), mid(MK, x)))
        mean = first / jnp.maximum(count, 1.0)

        def deviation(x):
            d = (mid(ref, x) - mean) * mid(MK, x)
            return (d * d,)

        (second,) = local_sum(deviation)
        return [first, second, count]

    def norm_exchange(k, q, ref, fill):
        rows = norm_begin(k, ref)
        sum_start(k, 0, rows)
        start_all(plane_copies(q, ref))
        rows = sum_wait(k, 0, True)
        sum_start(k, 1, rows)
        wait_all(plane_copies(q, ref))
        send_faces(q, ref)
        fill()
        wait_all(face_copies(q))
        rows = sum_wait(k, 1, True)
        mean = rows[0] / rows[2]
        rstd = lax.rsqrt(rows[1] / rows[2] + 1e-05)
        return mean, rstd, rows[2]

    wait_all(plane_copies(1, CT))
    send_faces(1, CT)
    mean1, rstd1, count = norm_exchange(0, 2, Y1, fill_weights)
    gain1, gain2, shift1, shift2 = GS[0:1], GS[1:2], GS[2:3], GS[3:4]

    def second_input(x, carry):
        def act(y, m):
            n = (y - mean1) * rstd1
            pre = gain1 * n + shift1
            return n, m * (pre * sigmoid(pre))

        n, hidden = act(Y1[x], MK[x])
        N1[x] = n
        faces = []
        for k in range(2):
            nf, hf = act(ZR[2, k, x], MZ[k, x])
            NZ1[k, x] = nf
            faces.append(hf)
        put(PH, x, hidden, faces[0], faces[1])
        return carry

    lax.fori_loop(0, XE, second_input, 0)

    def keep_y2(h, y):
        Y2[pl.ds(1 + h * H, H), 1 : 1 + Y, :, :] = y * own(MK, h)

    convolve(PH, W2, False, keep_y2)
    mean2, rstd2, _ = norm_exchange(1, 3, Y2, lambda: wait_all(face_copies(1)))

    def outgoing(y, s, m, ct):
        n = (y - mean2) * rstd2
        pre = gain2 * n + shift2 + s
        sig = sigmoid(pre)
        return n, m * (pre * sig), ct * m * (sig * (1.0 + pre * (1.0 - sig)))

    lane = lax.broadcasted_iota(jnp.int32, (1, L), 1)
    inner = jnp.where(lane < C, 1.0, 0.0).astype(F32)

    def last_forward(x, carry):
        n, out, d = outgoing(Y2[x], S[x] * inner, MK[x], CT[x])
        N2[x] = n
        D2[x] = d

        @pl.when((x >= 1) & (x <= X))
        def _():
            result_ref[x - 1] = out[1 : 1 + Y, :, 0:C].astype(BF16)

        for k in range(2):
            nf, _, df = outgoing(ZR[3, k, x], ZR[0, k, x] * inner, MZ[k, x], ZR[1, k, x])
            NZ2[k, x] = nf
            DZ2[k, x] = df
        return carry

    lax.fori_loop(0, XE, last_forward, 0)

    results = [pltpu.make_async_copy(result_ref, result_out, outs.at[0])]
    results[0].start()

    rows = local_sum(lambda x: (mid(D2, x), mid(D2, x) * mid(N2, x)))
    for part in range(2):
        sum_start(2, part, rows)
        rows = sum_wait(2, part, False)
    sum2, cross2 = rows

    def third_input(x, carry):
        factor = gain2 * rstd2

        def back(d, n, m):
            return m * factor * (d - sum2 / count - n * cross2 / count)

        main = back(D2[x], N2[x], MK[x])
        faces = [back(DZ2[k, x], NZ2[k, x], MZ[k, x]) for k in range(2)]
        put(PD2, x, main, faces[0], faces[1])
        return carry

    lax.fori_loop(0, XE, third_input, 0)

    def keep_d1(h, v):
        pre = gain1 * own(N1, h) + shift1
        sig = sigmoid(pre)
        D1[pl.ds(1 + h * H, H), 1 : 1 + Y, :, :] = (
            v * own(MK, h) * (sig * (1.0 + pre * (1.0 - sig)))
        )

    convolve(PD2, T2, True, keep_d1)
    rows = local_sum(lambda x: (mid(D1, x), mid(D1, x) * mid(N1, x)))
    sum_start(3, 0, rows)
    start_all(plane_copies(4, D1))
    prepare(PD2)
    products(1, PH, 0, 3)
    rows = sum_wait(3, 0, False)
    sum_start(3, 1, rows)
    wait_all(plane_copies(4, D1))
    send_faces(4, D1)
    products(1, PH, 3, 9)
    grad_step(1, 0)
    wait_all(face_copies(4))
    sum1, cross1 = sum_wait(3, 1, False)

    def fourth_input(x, carry):
        factor = gain1 * rstd1

        def back(d, n, m):
            return m * factor * (d - sum1 / count - n * cross1 / count)

        main = back(D1[x], N1[x], MK[x])
        faces = [back(ZR[4, k, x], NZ1[k, x], MZ[k, x]) for k in range(2)]
        put(PD1, x, main, faces[0], faces[1])
        return carry

    lax.fori_loop(0, XE, fourth_input, 0)
    grad_step(1, 1)
    prepare(PD1)
    products(0, PS, 0, 9)
    grad_step(0, 0)
    grad_step(1, 2)

    def keep_features(h, v):
        out = own(MK, h) * (own(D2, h) + v)
        gfeat_ref[pl.ds(h * H, H)] = out[:, :, :, 0:C].astype(BF16)

    convolve(PD1, T1, True, keep_features)
    at8 = lax.broadcasted_iota(jnp.int32, (8, L), 0)
    table = jnp.zeros((8, L), F32)
    for i, row in enumerate((cross1, sum1, cross2, sum2)):
        table = jnp.where(at8 == i, jnp.broadcast_to(row * scale, (8, L)), table)
    norm_ref[...] = table[0:4, 0:C]

    results.append(pltpu.make_async_copy(norm_ref, norm_out, outs.at[1]))
    results.append(pltpu.make_async_copy(gfeat_ref, gfeat_out, outs.at[2]))
    results[1].start()
    results[2].start()

    for stage in range(1, 8):
        grad_step(0, stage)
        if stage + 2 < 8:
            grad_step(1, stage + 2)
        if stage == 6:
            grad_store(1, g2_ref)
            results.append(pltpu.make_async_copy(g2_ref, g2_out, outs.at[3]))
            results[3].start()
    grad_store(0, g1_ref)
    results.append(pltpu.make_async_copy(g1_ref, g1_out, outs.at[4]))
    results[4].start()
    for c in results:
        c.wait()


def local(sizes, features, ground, thickness, weight_one, weight_two, gains, shifts, cotangent):
    NGX, NGY, NGZ = sizes
    X, Y, Z, C = features.shape
    n_y, n_z = NGZ // 2, NGX
    n = (n_y, n_z, NGY)
    pairs = [n[p] * n[(p + 1) % 3] for p in range(3)]
    tiles = -(-27 * C // (2 * 8 * min(pairs)))
    segs = tuple(8 * (tiles // 3 + (p < tiles % 3)) for p in range(3))
    dims = (NGX, NGY, NGZ, X, Y, Z, C, segs)
    XE, YE = X + 2, Y + 2
    ext = pltpu.VMEM((XE, YE, Z, L), F32)
    face = pltpu.VMEM((2, XE, YE, L), F32)
    patch = pltpu.VMEM((XE, YE, Z, 3 * L), BF16)
    weights = pltpu.VMEM((27 * L, L), BF16)
    dma = pltpu.SemaphoreType.DMA
    scratch = [
        pltpu.VMEM((X, Y, Z, C), BF16),
        pltpu.VMEM((X, Y, Z, C), BF16),
        pltpu.VMEM((27, C, C), BF16),
        pltpu.VMEM((27, C, C), BF16),
        pltpu.VMEM((2, C), F32),
        pltpu.VMEM((2, C), F32),
        pltpu.SMEM((X, Y), jnp.int32),
        pltpu.SMEM((X, Y), jnp.int32),
        pltpu.VMEM((X, Y, Z, C), BF16),
        pltpu.VMEM((X, Y, Z, C), BF16),
        pltpu.VMEM((27, C, C), F32),
        pltpu.VMEM((27, C, C), F32),
        pltpu.VMEM((4, C), F32),
    ]
    scratch += [ext] * 9
    scratch += [pltpu.VMEM((5, 2, XE, YE, L), F32)] * 2
    scratch += [face] * 4
    scratch += [pltpu.VMEM((YE, Z + 16, L), F32)]
    scratch += [patch] * 4
    scratch += [pltpu.VMEM((L, X * Y * Z), BF16)]
    scratch += [weights] * 4
    scratch += [pltpu.VMEM((8, L), F32)]
    n_a, n_b = 2 * n_z, NGY * n_y
    scratch += [pltpu.VMEM((4, 2, 4, L), F32)]
    scratch += [pltpu.VMEM((4, k, 4, L), F32) for k in (n_a, n_b)]
    len_c = sum(a * b for a, b in zip(pairs, segs))
    scratch += [
        pltpu.VMEM((2, 2 * len_c, L), F32),
        pltpu.VMEM((2, len_c, L), F32),
        pltpu.VMEM((2, 2 * len_c, L), F32),
    ]
    for p in range(3):
        n1, n2, n3 = n[p], n[(p + 1) % 3], n[(p + 2) % 3]
        seg = segs[p]
        scratch += [
            pltpu.VMEM((2, n1 * n2 * seg, L), F32),
            pltpu.VMEM((2, n1 - 1, n2 * seg, L), F32),
            pltpu.VMEM((2, n2 * seg, L), F32),
            pltpu.VMEM((2, n2 - 1, seg, L), F32),
            pltpu.VMEM((2, seg, L), F32),
            pltpu.VMEM((2, n3, seg, L), F32),
        ]
    most = max(n) - 1
    scratch += [dma((5, 8)), dma((5, 8)), dma((5, 2)), dma((5, 2))]
    scratch += [dma((n_a + n_b,)), dma((4, n_a + n_b))]
    scratch += [dma((2, 7, 3 * most)), dma((2, 7, 3 * most))]
    scratch += [dma((8,)), dma((5,))]
    anywhere = pl.BlockSpec(memory_space=pl.ANY)
    return pl.pallas_call(
        functools.partial(body, dims),
        out_shape=(
            jax.ShapeDtypeStruct((X, Y, Z, C), BF16),
            jax.ShapeDtypeStruct((X, Y, Z, C), BF16),
            jax.ShapeDtypeStruct((27, C, C), F32),
            jax.ShapeDtypeStruct((27, C, C), F32),
            jax.ShapeDtypeStruct((4, C), F32),
        ),
        in_specs=[anywhere] * 8,
        out_specs=(anywhere,) * 5,
        scratch_shapes=scratch,
        compiler_params=pltpu.CompilerParams(
            collective_id=0, has_side_effects=True, vmem_limit_bytes=62 * 1024 * 1024
        ),
    )(features, ground, thickness, weight_one, weight_two, gains, shifts, cotangent)


def solution(mesh):
    sizes = tuple(mesh.shape[a] for a in ("gx", "gy", "gz"))
    return jax.shard_map(
        functools.partial(local, sizes),
        mesh=mesh,
        in_specs=(
            P("gx", "gy", "gz", None),
            P("gx", "gy"),
            P("gx", "gy"),
            P(),
            P(),
            P(),
            P(),
            P("gx", "gy", "gz", None),
        ),
        out_specs=(P("gx", "gy", "gz", None), P("gx", "gy", "gz", None), P(), P(), P()),
        check_vma=False,
    )
```

```python
import functools
import math

import jax
import jax.numpy as jnp
from jax import lax
from jax.experimental import pallas as pl
from jax.experimental.pallas import tpu as pltpu
from jax.sharding import PartitionSpec as P

MESH = pl.DeviceIdType.MESH
F32 = jnp.float32
BF16 = jnp.bfloat16
L = 128
VMEM_BYTES = 63400000
SIDES = [(dx, dy) for dx in (-1, 0, 1) for dy in (-1, 0, 1) if (dx, dy) != (0, 0)]


def sigmoid(v):
    return 1.0 / (1.0 + jnp.exp(-v))


def body(
    dims,
    feat_in, ground_in, thick_in, w1_in, w2_in, gains_in, shifts_in, cot_in,
    result_out, gfeat_out, g1_out, g2_out, norm_out,
    feat_ref, cot_ref, w1_ref, w2_ref, gains_ref, shifts_ref, ground_ref, thick_ref,
    result_ref, gfeat_ref, g1_ref, g2_ref, norm_ref,
    HB, S, CT, Y1, Y2, D1, MK, N1, N2, D2,
    ZS, ZR, MZ, NZ1, NZ2, DZ2,
    V, PS, PH, PD2, PD1, DT, W1, W2, T1, T2, GS,
    STS, RA, RB,
    GA, GC, GF, *rest,
):
    NGX, NGY, NGZ, X, Y, Z, C, segs = dims
    portions = [rest[6 * p : 6 * p + 6] for p in range(3)]
    hs, hr, zs, zr, ss, sr, gs, gr, ins, outs = rest[18:]
    XE, YE = X + 2, Y + 2
    gx, gy, gz = lax.axis_index("gx"), lax.axis_index("gy"), lax.axis_index("gz")
    nz_lo, n_y = NGX // 2, NGZ // 2
    core, z_lo = gx % 2, gx // 2
    row_y, z_hi = gz // 2, gz % 2
    n_z = nz_lo * 2
    pos_z = z_hi * nz_lo + z_lo

    def dev(ax, ay, az):
        return (ax, ay, az)

    def peer_y(j):
        return dev(gx, (gy + j) % NGY, gz)

    def side(dx, dy):
        return dev((gx + dx + NGX) % NGX, (gy + dy + NGY) % NGY, gz)

    def grad_y(j):
        return dev(gx, gy, ((row_y + j) % n_y) * 2 + z_hi)

    def grad_z(j):
        other = (pos_z + j) % n_z
        return dev((other % nz_lo) * 2 + core, gy, row_y * 2 + other // nz_lo)

    partner = dev(z_lo * 2 + 1 - core, gy, gz)
    n_a, n_b = 2 * n_z, NGY * n_y
    me_a, me_b = pos_z * 2 + core, gy * n_y + row_y

    def peer_a(j):
        other = (me_a + j) % n_a
        pos = other // 2
        return dev((pos % nz_lo) * 2 + other % 2, gy, row_y * 2 + pos // nz_lo)

    def peer_b(j):
        other = (me_b + j) % n_b
        return dev(gx, other // n_y, (other % n_y) * 2 + z_hi)

    down = dev(gx, gy, (gz + NGZ - 1) % NGZ)
    up = dev(gx, gy, (gz + 1) % NGZ)

    greet = [peer_a(j) for j in range(1, n_a)]
    greet += [peer_b(j) for j in range(1, n_b)]
    greet += [down, up]
    greet += [side(dx, dy) for dx, dy in SIDES]
    barrier = pltpu.get_barrier_semaphore()
    for other in greet:
        pl.semaphore_signal(barrier, inc=1, device_id=other, device_id_type=MESH)

    arrivals = [
        pltpu.make_async_copy(src, dst, ins.at[i])
        for i, (src, dst) in enumerate(
            (
                (ground_in, ground_ref), (thick_in, thick_ref), (feat_in, feat_ref),
                (cot_in, cot_ref), (w1_in, w1_ref), (gains_in, gains_ref),
                (shifts_in, shifts_ref), (w2_in, w2_ref),
            )
        )
    ]
    for c in arrivals:
        c.start()

    for ref in (W1, W2, T1, T2, GS):
        ref[...] = jnp.zeros(ref.shape, ref.dtype)
    for c in arrivals[:4]:
        c.wait()

    def load_block(x, carry):
        level = lax.broadcasted_iota(jnp.int32, (Z, L), 0) + gz * Z
        for y in range(Y):
            low = ground_ref[x, y]
            high = low + thick_ref[x, y]
            m = jnp.where((level >= low) & (level < high), 1.0, 0.0).astype(F32)
            m = m.astype(BF16)
            HB[0, 1 + x, 1 + y] = m
            HB[0, 1 + x, 1 + y, :, 0:C] = m[:, 0:C] * feat_ref[x, y]
            HB[1, 1 + x, 1 + y] = jnp.zeros((Z, L), BF16)
            HB[1, 1 + x, 1 + y, :, 0:C] = cot_ref[x, y]
        return carry

    lax.fori_loop(0, X, load_block, 0)
    pl.semaphore_wait(barrier, len(greet))

    def cut(d, n, sending):
        if d == 0:
            return pl.ds(1, n)
        if sending:
            return pl.ds(n if d > 0 else 1, 1)
        return pl.ds(0 if d > 0 else n + 1, 1)

    def plane_copies(q):
        out = []
        for k, (dx, dy) in enumerate(SIDES):
            out.append(
                pltpu.make_async_remote_copy(
                    src_ref=HB.at[q, cut(dx, X, True), cut(dy, Y, True)],
                    dst_ref=HB.at[q, cut(dx, X, False), cut(dy, Y, False)],
                    send_sem=hs.at[q, k],
                    recv_sem=hr.at[q, k],
                    device_id=side(dx, dy),
                    device_id_type=MESH,
                )
            )
        return out

    def face_copies(q):
        out = []
        for k, other in ((0, down), (1, up)):
            out.append(
                pltpu.make_async_remote_copy(
                    src_ref=ZS.at[q, k],
                    dst_ref=ZR.at[q, 1 - k],
                    send_sem=zs.at[q, k],
                    recv_sem=zr.at[q, k],
                    device_id=other,
                    device_id_type=MESH,
                )
            )
        return out

    def start_all(copies):
        for c in copies:
            c.start()

    def wait_all(copies):
        for c in copies:
            c.wait()

    def send_faces(q, ref):
        if q > 1:
            for at in (0, XE - 1):
                ref[at] = HB[q, at].astype(F32)
            for at in (0, YE - 1):
                ref[1 : 1 + X, at] = HB[q, 1 : 1 + X, at].astype(F32)

        def one(x, carry):
            if q <= 1:
                ref[x] = HB[q, x].astype(F32)
            ZS[q, 0, x] = ref[x, :, 0, :].astype(BF16)
            ZS[q, 1, x] = ref[x, :, Z - 1, :].astype(BF16)
            return carry

        lax.fori_loop(0, XE, one, 0)
        start_all(face_copies(q))

    def sum_copies(k, part):
        n, me, peer, land = ((n_a, me_a, peer_a, RA), (n_b, me_b, peer_b, RB))[part]
        base = (0, n_a)[part]
        return [
            pltpu.make_async_remote_copy(
                src_ref=STS.at[k, part],
                dst_ref=land.at[k, me],
                send_sem=ss.at[base + j],
                recv_sem=sr.at[k, base + j],
                device_id=peer(j),
                device_id_type=MESH,
            )
            for j in range(1, n)
        ]

    def sum_start(k, part, rows):
        at = lax.broadcasted_iota(jnp.int32, (4, L), 0)
        tile = jnp.zeros((4, L), F32)
        for i, row in enumerate(rows):
            tile = jnp.where(at == i, jnp.broadcast_to(row, (4, L)), tile)
        STS[k, part] = tile
        me, land = ((me_a, RA), (me_b, RB))[part]
        land[k, me] = tile
        start_all(sum_copies(k, part))

    def sum_wait(k, part, spread):
        n, land = ((n_a, RA), (n_b, RB))[part]
        wait_all(sum_copies(k, part))
        tiles = land[k]
        first, second, third = (jnp.sum(tiles[:, i], axis=0, keepdims=True) for i in range(3))
        if not spread:
            return [first, second]
        mean = first / jnp.maximum(third, 1.0)
        each = tiles[:, 0] / jnp.maximum(tiles[:, 2], 1.0) - mean
        second = second + jnp.sum(tiles[:, 2] * each * each, axis=0, keepdims=True)
        return [first, second, third]

    def put(dest, x, main, low, high):
        V[:, 8 : 8 + Z, :] = main
        for y in range(YE):
            V[y, 7:8, :] = low[y : y + 1]
            V[y, 8 + Z : 9 + Z, :] = high[y : y + 1]
        for c in range(3):
            dest[x, :, :, c * L : (c + 1) * L] = V[:, 7 + c : 7 + c + Z, :].astype(BF16)

    H = X // 2

    def convolve(src, weights, flipped, finish):
        def half(h, carry):
            total = None
            for k0 in range(0, 9, 2):
                parts = []
                for k in range(k0, min(k0 + 2, 9)):
                    a, b = k // 3, k % 3
                    if flipped:
                        a, b = 2 - a, 2 - b
                    parts.append(
                        src[pl.ds(h * H + a, H), b : b + Y, :, :].reshape(H * Y * Z, 3 * L)
                    )
                left = jnp.concatenate(parts, axis=1) if len(parts) > 1 else parts[0]
                right = weights[k0 * 3 * L : (k0 * 3 + 3 * len(parts)) * L, :]
                term = jnp.dot(left, right, preferred_element_type=F32)
                total = term if total is None else total + term
            finish(h, total.reshape(H, Y, Z, L))
            return carry

        lax.fori_loop(0, 2, half, 0)

    def own(ref, h):
        return ref[pl.ds(1 + h * H, H), 1 : 1 + Y, :, :]

    def keep(q, ref, h, v):
        ref[pl.ds(1 + h * H, H), 1 : 1 + Y, :, :] = v
        HB[q, pl.ds(1 + h * H, H), 1 : 1 + Y, :, :] = v.astype(BF16)

    def local_sum(terms):
        def one(x, carry):
            return tuple(c + jnp.sum(t, axis=0) for c, t in zip(carry, terms(1 + x)))

        zero = tuple(jnp.zeros((Z, L), F32) for _ in terms(1))
        out = lax.fori_loop(0, X, one, zero)
        return [jnp.sum(v, axis=0, keepdims=True) for v in out]

    def mid(ref, x):
        return ref[x, 1 : 1 + Y, :, :]

    def prepare(dy):
        flat = dy[1 : 1 + X, 1 : 1 + Y, :, L : 2 * L].reshape(X * Y * Z, L)
        DT[...] = flat.T

    def products(g, src, first, last):
        def one(k, carry):
            a, b = k // 3, k % 3
            patch = src[pl.ds(a, X), pl.ds(b, Y), :, :].reshape(X * Y * Z, 3 * L)
            out = jnp.dot(DT[...], patch, preferred_element_type=F32)
            for c in range(3):
                GA[g, pl.ds(pl.multiple_of((3 * k + c) * C, 8), C), :] = (
                    out[:, c * L : (c + 1) * L].T[0:C]
                )
            return carry

        lax.fori_loop(first, last, one, 0)

    axes = ((n_y, row_y, grad_y), (n_z, pos_z, grad_z), (NGY, gy, peer_y))
    plans = []
    base = 0
    for p in range(3):
        plan = [axes[(p + i) % 3] for i in range(3)]
        len1 = plan[1][0] * segs[p]
        plans.append((plan, base, len1, segs[p]))
        base += plan[0][0] * len1
    len_c = base

    def rows_at(off, n):
        return pl.ds(pl.multiple_of(off, 8), n)

    most = max(n_y, n_z, NGY) - 1

    def grad_copies(g, stage):
        def copy(src, dst, k, other):
            return pltpu.make_async_remote_copy(
                src_ref=src, dst_ref=dst, send_sem=gs.at[g, stage, k],
                recv_sem=gr.at[g, stage, k], device_id=other, device_id_type=MESH,
            )

        if stage == 0:
            return [copy(GA.at[g, rows_at((1 - core) * len_c, len_c)], GC.at[g], 0, partner)]
        if stage == 6:
            part = GF.at[g, rows_at(core * len_c, len_c)]
            return [copy(part, part, 0, partner)]
        out = []
        for p, (plan, base, len1, seg) in enumerate(plans):
            GB, GY, GD, GZ, GE, GX = portions[p]
            n, me, peer = plan[(None, 0, 1, 2, 1, 0)[stage]]
            off1 = core * len_c + base + plan[0][1] * len1
            off2 = off1 + plan[1][1] * seg
            for j in range(1, n):
                if stage == 1:
                    part = GB.at[g, rows_at(((me + j) % n) * len1, len1)]
                    land = GY.at[g, j - 1]
                elif stage == 2:
                    part = GD.at[g, rows_at(((me + j) % n) * seg, seg)]
                    land = GZ.at[g, j - 1]
                elif stage == 3:
                    part, land = GE.at[g], GX.at[g, me]
                elif stage == 4:
                    part = land = GF.at[g, rows_at(off2, seg)]
                else:
                    part = land = GF.at[g, rows_at(off1, len1)]
                out.append(copy(part, land, p * most + j - 1, peer(j)))
        return out

    def grad_step(g, stage):
        if stage > 0:
            wait_all(grad_copies(g, stage - 1))
        for p, (plan, base, len1, seg) in enumerate(plans):
            GB, GY, GD, GZ, GE, GX = portions[p]
            if stage == 1:
                def fold(i, carry):
                    at = i * len1 + base
                    GB[g, rows_at(i * len1, len1)] = (
                        GA[g, rows_at(core * len_c + at, len1)] + GC[g, rows_at(at, len1)]
                    )
                    return carry

                lax.fori_loop(0, plan[0][0], fold, 0)
            if stage == 2:
                v = GB[g, rows_at(plan[0][1] * len1, len1)]
                for j in range(plan[0][0] - 1):
                    v = v + GY[g, j]
                GD[g] = v
            if stage == 3:
                v = GD[g, rows_at(plan[1][1] * seg, seg)]
                for j in range(plan[1][0] - 1):
                    v = v + GZ[g, j]
                GE[g] = v
                GX[g, plan[2][1]] = v
            if stage == 4:
                v = GX[g, 0]
                for j in range(1, plan[2][0]):
                    v = v + GX[g, j]
                off = core * len_c + base + plan[0][1] * len1 + plan[1][1] * seg
                GF[g, rows_at(off, seg)] = v
        if stage < 7:
            start_all(grad_copies(g, stage))

    total_cells = X * NGX * Y * NGY * Z * NGZ
    scale = 1.0 / math.sqrt(total_cells / 8.0)

    def grad_store(g, out_ref):
        def one(t, carry):
            out_ref[t] = GF[g, rows_at(t * C, C)][:, 0:C] * scale
            return carry

        lax.fori_loop(0, 27, one, 0)

    start_all(plane_copies(0))
    for c in arrivals[4:7]:
        c.wait()
    GS[0:2, 0:C] = gains_ref[...]
    GS[2:4, 0:C] = shifts_ref[...]

    def load_first(t, carry):
        W1[pl.ds(pl.multiple_of(t * L, L), C), 0:C] = w1_ref[t]
        return carry

    lax.fori_loop(0, 27, load_first, 0)

    def load_rest(t, carry):
        W2[pl.ds(pl.multiple_of(t * L, L), C), 0:C] = w2_ref[t]
        whole = pl.ds(pl.multiple_of(t * L, L), L)
        back = pl.ds(pl.multiple_of((t - t % 3 + 2 - t % 3) * L, L), L)
        T1[back, :] = W1[whole, :].T
        T2[back, :] = W2[whole, :].T
        return carry

    def fill_weights():
        arrivals[7].wait()
        lax.fori_loop(0, 27, load_rest, 0)

    wait_all(plane_copies(0))
    send_faces(0, S)
    wait_all(face_copies(0))
    start_all(plane_copies(1))

    at_y = lax.broadcasted_iota(jnp.int32, (YE, L), 0)
    live_y = jnp.where(
        ((at_y == 0) & (gy == 0)) | ((at_y == YE - 1) & (gy == NGY - 1)), 0.0, 1.0
    ).astype(F32)
    live_z = [jnp.where(gz == 0, 0.0, 1.0), jnp.where(gz == NGZ - 1, 0.0, 1.0)]

    def spread_lanes(v):
        return jnp.broadcast_to(v[..., L - 1 : L], v.shape)

    def first_input(x, carry):
        gone = ((x == 0) & (gx == 0)) | ((x == XE - 1) & (gx == NGX - 1))
        live = live_y * jnp.where(gone, 0.0, 1.0)
        s = S[x]
        m = spread_lanes(s) * live[:, None, :]
        MK[x] = m
        s = s * m
        S[x] = s
        faces = []
        for k in range(2):
            f = ZR[0, k, x].astype(F32)
            mf = spread_lanes(f) * (live * live_z[k])
            MZ[k, x] = mf
            f = f * mf
            ZR[0, k, x] = f.astype(BF16)
            faces.append(f)
        put(PS, x, s, faces[0], faces[1])
        return carry

    lax.fori_loop(0, XE, first_input, 0)

    def keep_y1(h, y):
        keep(2, Y1, h, y * own(MK, h))

    convolve(PS, W1, False, keep_y1)

    def norm_begin(k, ref):
        first, count = local_sum(lambda x: (mid(ref, x), mid(MK, x)))
        mean = first / jnp.maximum(count, 1.0)

        def deviation(x):
            d = (mid(ref, x) - mean) * mid(MK, x)
            return (d * d,)

        (second,) = local_sum(deviation)
        return [first, second, count]

    def norm_exchange(k, q, ref, fill):
        rows = norm_begin(k, ref)
        sum_start(k, 0, rows)
        start_all(plane_copies(q))
        rows = sum_wait(k, 0, True)
        sum_start(k, 1, rows)
        wait_all(plane_copies(q))
        send_faces(q, ref)
        fill()
        wait_all(face_copies(q))
        rows = sum_wait(k, 1, True)
        mean = rows[0] / rows[2]
        rstd = lax.rsqrt(rows[1] / rows[2] + 1e-05)
        return mean, rstd, rows[2]

    wait_all(plane_copies(1))
    send_faces(1, CT)
    mean1, rstd1, count = norm_exchange(0, 2, Y1, fill_weights)
    gain1, gain2, shift1, shift2 = GS[0:1], GS[1:2], GS[2:3], GS[3:4]

    def second_input(x, carry):
        def act(y, m):
            n = (y - mean1) * rstd1
            pre = gain1 * n + shift1
            return n, m * (pre * sigmoid(pre))

        n, hidden = act(Y1[x], MK[x])
        N1[x] = n
        faces = []
        for k in range(2):
            nf, hf = act(ZR[2, k, x].astype(F32), MZ[k, x])
            NZ1[k, x] = nf
            faces.append(hf)
        put(PH, x, hidden, faces[0], faces[1])
        return carry

    lax.fori_loop(0, XE, second_input, 0)

    def keep_y2(h, y):
        keep(3, Y2, h, y * own(MK, h))

    convolve(PH, W2, False, keep_y2)
    mean2, rstd2, _ = norm_exchange(1, 3, Y2, lambda: wait_all(face_copies(1)))

    def outgoing(y, s, m, ct):
        n = (y - mean2) * rstd2
        pre = gain2 * n + shift2 + s
        sig = sigmoid(pre)
        return n, m * (pre * sig), ct * m * (sig * (1.0 + pre * (1.0 - sig)))

    lane = lax.broadcasted_iota(jnp.int32, (1, L), 1)
    inner = jnp.where(lane < C, 1.0, 0.0).astype(F32)

    def last_forward(x, carry):
        n, out, d = outgoing(Y2[x], S[x] * inner, MK[x], CT[x])
        N2[x] = n
        D2[x] = d

        @pl.when((x >= 1) & (x <= X))
        def _():
            result_ref[x - 1] = out[1 : 1 + Y, :, 0:C].astype(BF16)

        for k in range(2):
            y, s, ct = (ZR[q, k, x].astype(F32) for q in (3, 0, 1))
            nf, _, df = outgoing(y, s * inner, MZ[k, x], ct)
            NZ2[k, x] = nf
            DZ2[k, x] = df
        return carry

    lax.fori_loop(0, XE, last_forward, 0)

    results = [pltpu.make_async_copy(result_ref, result_out, outs.at[0])]
    results[0].start()

    rows = local_sum(lambda x: (mid(D2, x), mid(D2, x) * mid(N2, x)))
    for part in range(2):
        sum_start(2, part, rows)
        rows = sum_wait(2, part, False)
    sum2, cross2 = rows

    def third_input(x, carry):
        factor = gain2 * rstd2

        def back(d, n, m):
            return m * factor * (d - sum2 / count - n * cross2 / count)

        main = back(D2[x], N2[x], MK[x])
        faces = [back(DZ2[k, x], NZ2[k, x], MZ[k, x]) for k in range(2)]
        put(PD2, x, main, faces[0], faces[1])
        return carry

    lax.fori_loop(0, XE, third_input, 0)

    def keep_d1(h, v):
        pre = gain1 * own(N1, h) + shift1
        sig = sigmoid(pre)
        keep(4, D1, h, v * own(MK, h) * (sig * (1.0 + pre * (1.0 - sig))))

    convolve(PD2, T2, True, keep_d1)
    rows = local_sum(lambda x: (mid(D1, x), mid(D1, x) * mid(N1, x)))
    sum_start(3, 0, rows)
    start_all(plane_copies(4))
    prepare(PD2)
    products(1, PH, 0, 3)
    rows = sum_wait(3, 0, False)
    sum_start(3, 1, rows)
    wait_all(plane_copies(4))
    send_faces(4, D1)
    products(1, PH, 3, 9)
    grad_step(1, 0)
    wait_all(face_copies(4))
    sum1, cross1 = sum_wait(3, 1, False)

    def fourth_input(x, carry):
        factor = gain1 * rstd1

        def back(d, n, m):
            return m * factor * (d - sum1 / count - n * cross1 / count)

        main = back(D1[x], N1[x], MK[x])
        faces = [back(ZR[4, k, x].astype(F32), NZ1[k, x], MZ[k, x]) for k in range(2)]
        put(PD1, x, main, faces[0], faces[1])
        return carry

    lax.fori_loop(0, XE, fourth_input, 0)
    grad_step(1, 1)
    prepare(PD1)
    products(0, PS, 0, 9)
    grad_step(0, 0)
    grad_step(1, 2)

    def keep_features(h, v):
        out = own(MK, h) * (own(D2, h) + v)
        gfeat_ref[pl.ds(h * H, H)] = out[:, :, :, 0:C].astype(BF16)

    convolve(PD1, T1, True, keep_features)
    at8 = lax.broadcasted_iota(jnp.int32, (8, L), 0)
    table = jnp.zeros((8, L), F32)
    for i, row in enumerate((cross1, sum1, cross2, sum2)):
        table = jnp.where(at8 == i, jnp.broadcast_to(row * scale, (8, L)), table)
    norm_ref[...] = table[0:4, 0:C]

    results.append(pltpu.make_async_copy(norm_ref, norm_out, outs.at[1]))
    results.append(pltpu.make_async_copy(gfeat_ref, gfeat_out, outs.at[2]))
    results[1].start()
    results[2].start()

    for stage in range(1, 8):
        grad_step(0, stage)
        if stage + 2 < 8:
            grad_step(1, stage + 2)
        if stage == 6:
            grad_store(1, g2_ref)
            results.append(pltpu.make_async_copy(g2_ref, g2_out, outs.at[3]))
            results[3].start()
    grad_store(0, g1_ref)
    results.append(pltpu.make_async_copy(g1_ref, g1_out, outs.at[4]))
    results[4].start()
    for c in results:
        c.wait()


def hand_over(*refs):
    ins, outs, held, (into, out) = refs[0:5], refs[5:10], refs[10:15], refs[15:17]
    first = [pltpu.make_async_copy(a, b, into.at[i]) for i, (a, b) in enumerate(zip(ins, held))]
    last = [pltpu.make_async_copy(a, b, out.at[i]) for i, (a, b) in enumerate(zip(held, outs))]
    for c in first:
        c.start()
    for a, b in zip(first, last):
        a.wait()
        b.start()
    for c in last:
        c.wait()


def local(sizes, features, ground, thickness, weight_one, weight_two, gains, shifts, cotangent):
    NGX, NGY, NGZ = sizes
    X, Y, Z, C = features.shape
    n_y, n_z = NGZ // 2, NGX
    n = (n_y, n_z, NGY)
    pairs = [n[p] * n[(p + 1) % 3] for p in range(3)]
    tiles = -(-27 * C // (2 * 8 * min(pairs)))
    segs = tuple(8 * (tiles // 3 + (p < tiles % 3)) for p in range(3))
    dims = (NGX, NGY, NGZ, X, Y, Z, C, segs)
    XE, YE = X + 2, Y + 2
    ext = pltpu.VMEM((XE, YE, Z, L), F32)
    face = pltpu.VMEM((2, XE, YE, L), F32)
    patch = pltpu.VMEM((XE, YE, Z, 3 * L), BF16)
    weights = pltpu.VMEM((27 * L, L), BF16)
    dma = pltpu.SemaphoreType.DMA
    scratch = [
        pltpu.VMEM((X, Y, Z, C), BF16),
        pltpu.VMEM((X, Y, Z, C), BF16),
        pltpu.VMEM((27, C, C), BF16),
        pltpu.VMEM((27, C, C), BF16),
        pltpu.VMEM((2, C), F32),
        pltpu.VMEM((2, C), F32),
        pltpu.SMEM((X, Y), jnp.int32),
        pltpu.SMEM((X, Y), jnp.int32),
        pltpu.VMEM((X, Y, Z, C), BF16),
        pltpu.VMEM((X, Y, Z, C), BF16),
        pltpu.VMEM((27, C, C), F32),
        pltpu.VMEM((27, C, C), F32),
        pltpu.VMEM((4, C), F32),
    ]
    scratch += [pltpu.VMEM((5, XE, YE, Z, L), BF16)]
    scratch += [ext] * 9
    scratch += [pltpu.VMEM((5, 2, XE, YE, L), BF16)] * 2
    scratch += [face] * 4
    scratch += [pltpu.VMEM((YE, Z + 16, L), F32)]
    scratch += [patch] * 4
    scratch += [pltpu.VMEM((L, X * Y * Z), BF16)]
    scratch += [weights] * 4
    scratch += [pltpu.VMEM((8, L), F32)]
    n_a, n_b = 2 * n_z, NGY * n_y
    scratch += [pltpu.VMEM((4, 2, 4, L), F32)]
    scratch += [pltpu.VMEM((4, k, 4, L), F32) for k in (n_a, n_b)]
    len_c = sum(a * b for a, b in zip(pairs, segs))
    scratch += [
        pltpu.VMEM((2, 2 * len_c, L), F32),
        pltpu.VMEM((2, len_c, L), F32),
        pltpu.VMEM((2, 2 * len_c, L), F32),
    ]
    for p in range(3):
        n1, n2, n3 = n[p], n[(p + 1) % 3], n[(p + 2) % 3]
        seg = segs[p]
        scratch += [
            pltpu.VMEM((2, n1 * n2 * seg, L), F32),
            pltpu.VMEM((2, n1 - 1, n2 * seg, L), F32),
            pltpu.VMEM((2, n2 * seg, L), F32),
            pltpu.VMEM((2, n2 - 1, seg, L), F32),
            pltpu.VMEM((2, seg, L), F32),
            pltpu.VMEM((2, n3, seg, L), F32),
        ]
    most = max(n) - 1
    scratch += [dma((5, 8)), dma((5, 8)), dma((5, 2)), dma((5, 2))]
    scratch += [dma((n_a + n_b,)), dma((4, n_a + n_b))]
    scratch += [dma((2, 7, 3 * most)), dma((2, 7, 3 * most))]
    scratch += [dma((8,)), dma((5,))]
    anywhere = pl.BlockSpec(memory_space=pl.ANY)
    shapes = (
        jax.ShapeDtypeStruct((X, Y, Z, C), BF16),
        jax.ShapeDtypeStruct((X, Y, Z, C), BF16),
        jax.ShapeDtypeStruct((27, C, C), F32),
        jax.ShapeDtypeStruct((27, C, C), F32),
        jax.ShapeDtypeStruct((4, C), F32),
    )
    outs = pl.pallas_call(
        functools.partial(body, dims),
        out_shape=shapes,
        in_specs=[pl.BlockSpec(memory_space=pltpu.HBM)] * 8,
        out_specs=(anywhere,) * 5,
        scratch_shapes=scratch,
        compiler_params=pltpu.CompilerParams(
            collective_id=0, has_side_effects=True, vmem_limit_bytes=VMEM_BYTES
        ),
    )(features, ground, thickness, weight_one, weight_two, gains, shifts, cotangent)
    return pl.pallas_call(
        hand_over,
        out_shape=shapes,
        in_specs=[anywhere] * 5,
        out_specs=(pl.BlockSpec(memory_space=pltpu.HBM),) * 5,
        scratch_shapes=[pltpu.VMEM(v.shape, v.dtype) for v in shapes] + [dma((5,)), dma((5,))],
        compiler_params=pltpu.CompilerParams(vmem_limit_bytes=VMEM_BYTES),
    )(*outs)


def solution(mesh):
    sizes = tuple(mesh.shape[a] for a in ("gx", "gy", "gz"))
    return jax.shard_map(
        functools.partial(local, sizes),
        mesh=mesh,
        in_specs=(
            P("gx", "gy", "gz", None),
            P("gx", "gy"),
            P("gx", "gy"),
            P(),
            P(),
            P(),
            P(),
            P("gx", "gy", "gz", None),
        ),
        out_specs=(P("gx", "gy", "gz", None), P("gx", "gy", "gz", None), P(), P(), P()),
        check_vma=False,
    )
```

```python
import functools
import math

import jax
import jax.numpy as jnp
from jax import lax
from jax.experimental import pallas as pl
from jax.experimental.pallas import tpu as pltpu
from jax.sharding import PartitionSpec as P

MESH = pl.DeviceIdType.MESH
F32 = jnp.float32
BF16 = jnp.bfloat16
L = 128
VMEM_BYTES = 63400000
SIDES = [(dx, dy) for dx in (-1, 0, 1) for dy in (-1, 0, 1) if (dx, dy) != (0, 0)]


def sigmoid(v):
    return 1.0 / (1.0 + jnp.exp(-v))


def body(
    dims,
    feat_in, ground_in, thick_in, w1_in, w2_in, gains_in, shifts_in, cot_in,
    result_out, gfeat_out, g1_out, g2_out, norm_out,
    feat_ref, cot_ref, w1_ref, w2_ref, gains_ref, shifts_ref, ground_ref, thick_ref,
    result_ref, gfeat_ref, g1_ref, g2_ref, norm_ref,
    HB, S, CT, Y1, Y2, D1, MK, N1, N2, D2,
    ZS, ZR, MZ, NZ1, NZ2, DZ2,
    V, PS, PH, PD2, PD1, DT, W1, W2, T1, T2, GS,
    STS, RA, RB,
    GA, GC, GF, *rest,
):
    NGX, NGY, NGZ, X, Y, Z, C, segs = dims
    portions = [rest[6 * p : 6 * p + 6] for p in range(3)]
    hs, hr, zs, zr, ss, sr, gs, gr, ins, outs = rest[18:]
    XE, YE = X + 2, Y + 2
    gx, gy, gz = lax.axis_index("gx"), lax.axis_index("gy"), lax.axis_index("gz")
    nz_lo, n_y = NGX // 2, NGZ // 2
    core, z_lo = gx % 2, gx // 2
    row_y, z_hi = gz // 2, gz % 2
    n_z = nz_lo * 2
    pos_z = z_hi * nz_lo + z_lo

    def dev(ax, ay, az):
        return (ax, ay, az)

    def peer_y(j):
        return dev(gx, (gy + j) % NGY, gz)

    def side(dx, dy):
        return dev((gx + dx + NGX) % NGX, (gy + dy + NGY) % NGY, gz)

    def grad_y(j):
        return dev(gx, gy, ((row_y + j) % n_y) * 2 + z_hi)

    def grad_z(j):
        other = (pos_z + j) % n_z
        return dev((other % nz_lo) * 2 + core, gy, row_y * 2 + other // nz_lo)

    partner = dev(z_lo * 2 + 1 - core, gy, gz)
    n_a, n_b = 2 * n_z, NGY * n_y
    me_a, me_b = pos_z * 2 + core, gy * n_y + row_y

    def peer_a(j):
        other = (me_a + j) % n_a
        pos = other // 2
        return dev((pos % nz_lo) * 2 + other % 2, gy, row_y * 2 + pos // nz_lo)

    def peer_b(j):
        other = (me_b + j) % n_b
        return dev(gx, other // n_y, (other % n_y) * 2 + z_hi)

    down = dev(gx, gy, (gz + NGZ - 1) % NGZ)
    up = dev(gx, gy, (gz + 1) % NGZ)

    greet = [peer_a(j) for j in range(1, n_a)]
    greet += [peer_b(j) for j in range(1, n_b)]
    greet += [down, up]
    greet += [side(dx, dy) for dx, dy in SIDES]
    barrier = pltpu.get_barrier_semaphore()
    for other in greet:
        pl.semaphore_signal(barrier, inc=1, device_id=other, device_id_type=MESH)

    arrivals = [
        pltpu.make_async_copy(src, dst, ins.at[i])
        for i, (src, dst) in enumerate(
            (
                (ground_in, ground_ref), (thick_in, thick_ref), (feat_in, feat_ref),
                (cot_in, cot_ref), (w1_in, w1_ref), (gains_in, gains_ref),
                (shifts_in, shifts_ref), (w2_in, w2_ref),
            )
        )
    ]
    for c in arrivals:
        c.start()

    for ref in (W1, W2, T1, T2, GS):
        ref[...] = jnp.zeros(ref.shape, ref.dtype)
    for c in arrivals[:4]:
        c.wait()

    def load_block(x, carry):
        level = lax.broadcasted_iota(jnp.int32, (Z, L), 0) + gz * Z
        for y in range(Y):
            low = ground_ref[x, y]
            high = low + thick_ref[x, y]
            m = jnp.where((level >= low) & (level < high), 1.0, 0.0).astype(F32)
            m = m.astype(BF16)
            HB[0, 1 + x, 1 + y] = m
            HB[0, 1 + x, 1 + y, :, 0:C] = m[:, 0:C] * feat_ref[x, y]
            HB[1, 1 + x, 1 + y] = jnp.zeros((Z, L), BF16)
            HB[1, 1 + x, 1 + y, :, 0:C] = cot_ref[x, y]
        return carry

    lax.fori_loop(0, X, load_block, 0)
    pl.semaphore_wait(barrier, len(greet))

    def cut(d, n, sending):
        if d == 0:
            return pl.ds(1, n)
        if sending:
            return pl.ds(n if d > 0 else 1, 1)
        return pl.ds(0 if d > 0 else n + 1, 1)

    def plane_copies(q):
        out = []
        for k, (dx, dy) in enumerate(SIDES):
            out.append(
                pltpu.make_async_remote_copy(
                    src_ref=HB.at[q, cut(dx, X, True), cut(dy, Y, True)],
                    dst_ref=HB.at[q, cut(dx, X, False), cut(dy, Y, False)],
                    send_sem=hs.at[q, k],
                    recv_sem=hr.at[q, k],
                    device_id=side(dx, dy),
                    device_id_type=MESH,
                )
            )
        return out

    def face_copies(q):
        out = []
        for k, other in ((0, down), (1, up)):
            out.append(
                pltpu.make_async_remote_copy(
                    src_ref=ZS.at[q, k],
                    dst_ref=ZR.at[q, 1 - k],
                    send_sem=zs.at[q, k],
                    recv_sem=zr.at[q, k],
                    device_id=other,
                    device_id_type=MESH,
                )
            )
        return out

    def start_all(copies):
        for c in copies:
            c.start()

    def wait_all(copies):
        for c in copies:
            c.wait()

    def send_faces(q, ref):
        if q > 1:
            for at in (0, XE - 1):
                ref[at] = HB[q, at].astype(F32)
            for at in (0, YE - 1):
                ref[1 : 1 + X, at] = HB[q, 1 : 1 + X, at].astype(F32)

        def one(x, carry):
            if q <= 1:
                ref[x] = HB[q, x].astype(F32)
            ZS[q, 0, x] = ref[x, :, 0, :].astype(BF16)
            ZS[q, 1, x] = ref[x, :, Z - 1, :].astype(BF16)
            return carry

        lax.fori_loop(0, XE, one, 0)
        start_all(face_copies(q))

    def sum_copies(k, part):
        n, me, peer, land = ((n_a, me_a, peer_a, RA), (n_b, me_b, peer_b, RB))[part]
        base = (0, n_a)[part]
        return [
            pltpu.make_async_remote_copy(
                src_ref=STS.at[k, part],
                dst_ref=land.at[k, me],
                send_sem=ss.at[base + j],
                recv_sem=sr.at[k, base + j],
                device_id=peer(j),
                device_id_type=MESH,
            )
            for j in range(1, n)
        ]

    def sum_start(k, part, rows):
        at = lax.broadcasted_iota(jnp.int32, (4, L), 0)
        tile = jnp.zeros((4, L), F32)
        for i, row in enumerate(rows):
            tile = jnp.where(at == i, jnp.broadcast_to(row, (4, L)), tile)
        STS[k, part] = tile
        me, land = ((me_a, RA), (me_b, RB))[part]
        land[k, me] = tile
        start_all(sum_copies(k, part))

    def sum_wait(k, part, spread):
        n, land = ((n_a, RA), (n_b, RB))[part]
        wait_all(sum_copies(k, part))
        tiles = land[k]
        first, second, third = (jnp.sum(tiles[:, i], axis=0, keepdims=True) for i in range(3))
        if not spread:
            return [first, second]
        mean = first / jnp.maximum(third, 1.0)
        each = tiles[:, 0] / jnp.maximum(tiles[:, 2], 1.0) - mean
        second = second + jnp.sum(tiles[:, 2] * each * each, axis=0, keepdims=True)
        return [first, second, third]

    def put(dest, x, main, low, high):
        V[:, 8 : 8 + Z, :] = main
        for y in range(YE):
            V[y, 7:8, :] = low[y : y + 1]
            V[y, 8 + Z : 9 + Z, :] = high[y : y + 1]
        for c in range(3):
            dest[x, :, :, c * L : (c + 1) * L] = V[:, 7 + c : 7 + c + Z, :].astype(BF16)

    H = X // 2

    def convolve(src, weights, flipped, finish):
        def half(h, carry):
            total = None
            for k0 in range(0, 9, 2):
                parts = []
                for k in range(k0, min(k0 + 2, 9)):
                    a, b = k // 3, k % 3
                    if flipped:
                        a, b = 2 - a, 2 - b
                    parts.append(
                        src[pl.ds(h * H + a, H), b : b + Y, :, :].reshape(H * Y * Z, 3 * L)
                    )
                left = jnp.concatenate(parts, axis=1) if len(parts) > 1 else parts[0]
                right = weights[k0 * 3 * L : (k0 * 3 + 3 * len(parts)) * L, :]
                term = jnp.dot(left, right, preferred_element_type=F32)
                total = term if total is None else total + term
            finish(h, total.reshape(H, Y, Z, L))
            return carry

        lax.fori_loop(0, 2, half, 0)

    def own(ref, h):
        return ref[pl.ds(1 + h * H, H), 1 : 1 + Y, :, :]

    def keep(q, ref, h, v):
        ref[pl.ds(1 + h * H, H), 1 : 1 + Y, :, :] = v
        HB[q, pl.ds(1 + h * H, H), 1 : 1 + Y, :, :] = v.astype(BF16)

    def local_sum(terms):
        def one(x, carry):
            return tuple(c + jnp.sum(t, axis=0) for c, t in zip(carry, terms(1 + x)))

        zero = tuple(jnp.zeros((Z, L), F32) for _ in terms(1))
        out = lax.fori_loop(0, X, one, zero)
        return [jnp.sum(v, axis=0, keepdims=True) for v in out]

    def mid(ref, x):
        return ref[x, 1 : 1 + Y, :, :]

    def prepare(get):
        for x in range(X):
            DT[:, x * Y * Z : (x + 1) * Y * Z] = get(1 + x).reshape(Y * Z, L).astype(BF16).T

    def products(g, src, first, last):
        def one(k, carry):
            a, b = k // 3, k % 3
            patch = src[pl.ds(a, X), pl.ds(b, Y), :, :].reshape(X * Y * Z, 3 * L)
            out = jnp.dot(DT[...], patch, preferred_element_type=F32)
            for c in range(3):
                GA[g, pl.ds(pl.multiple_of((3 * k + c) * C, 16), C), :] = (
                    out[:, c * L : (c + 1) * L].T[0:C]
                )
            return carry

        lax.fori_loop(first, last, one, 0)

    axes = ((n_y, row_y, grad_y), (n_z, pos_z, grad_z), (NGY, gy, peer_y))
    plans = []
    base = 0
    for p in range(3):
        plan = [axes[(p + i) % 3] for i in range(3)]
        len1 = plan[1][0] * segs[p]
        plans.append((plan, base, len1, segs[p]))
        base += plan[0][0] * len1
    len_c = base

    def rows_at(off, n):
        return pl.ds(pl.multiple_of(off, 16), n)

    most = max(n_y, n_z, NGY) - 1

    def grad_copies(g, stage):
        def copy(src, dst, k, other):
            return pltpu.make_async_remote_copy(
                src_ref=src, dst_ref=dst, send_sem=gs.at[g, k],
                recv_sem=gr.at[g * 7 + stage if g < 2 else 6 + g * 4 + stage, k], device_id=other, device_id_type=MESH,
            )

        if stage == 0:
            return [copy(GA.at[g, rows_at((1 - core) * len_c, len_c)], GC.at[g], 0, partner)]
        if stage == 6:
            part = GF.at[g, rows_at(core * len_c, len_c)]
            return [copy(part, part, 0, partner)]
        out = []
        for p, (plan, base, len1, seg) in enumerate(plans):
            GB, GY, GD, GZ, GE, GX = portions[p]
            n, me, peer = plan[(None, 0, 1, 2, 1, 0)[stage]]
            off1 = core * len_c + base + plan[0][1] * len1
            off2 = off1 + plan[1][1] * seg
            for j in range(1, n):
                if stage == 1:
                    part = GB.at[g, rows_at(((me + j) % n) * len1, len1)]
                    land = GY.at[g, j - 1]
                elif stage == 2:
                    part = GD.at[g, rows_at(((me + j) % n) * seg, seg)]
                    land = GZ.at[g, j - 1]
                elif stage == 3:
                    part, land = GE.at[g], GX.at[g, me]
                elif stage == 4:
                    part = land = GF.at[g, rows_at(off2, seg)]
                else:
                    part = land = GF.at[g, rows_at(off1, len1)]
                out.append(copy(part, land, p * most + j - 1, peer(j)))
        return out

    def grad_step(g, stage, late=None):
        if stage > 0:
            wait_all(grad_copies(g, stage - 1))
        if stage == 4:
            wait_all(grad_copies(g + 2, 3))
        for p, (plan, base, len1, seg) in enumerate(plans):
            GB, GY, GD, GZ, GE, GX = portions[p]
            if stage == 1:
                def fold(i, carry):
                    at = i * len1 + base
                    GB[g, rows_at(i * len1, len1)] = (
                        GA[g, rows_at(core * len_c + at, len1)] + GC[g, rows_at(at, len1)]
                    )
                    return carry

                lax.fori_loop(0, plan[0][0], fold, 0)
            if stage == 2:
                v = GB[g, rows_at(plan[0][1] * len1, len1)]
                for j in range(plan[0][0] - 1):
                    v = v + GY[g, j]
                GD[g] = v
            if stage == 3:
                v = GD[g, rows_at(plan[1][1] * seg, seg)]
                for j in range(plan[1][0] - 1):
                    v = v + GZ[g, j]
                GE[g] = v
                GX[g, plan[2][1]] = v
            if stage == 4:
                v, w = GX[g, 0], GX[g + 2, 0]
                for j in range(1, plan[2][0]):
                    v = v + GX[g, j]
                    w = w + GX[g + 2, j]
                total, cross, factor = late
                v = factor * (v - (total / count) * spread_lanes(w) - (cross / count) * w)
                off = core * len_c + base + plan[0][1] * len1 + plan[1][1] * seg
                GF[g, rows_at(off, seg)] = v.astype(BF16)
        if stage < 7:
            start_all(grad_copies(g, stage))

    total_cells = X * NGX * Y * NGY * Z * NGZ
    scale = 1.0 / math.sqrt(total_cells / 8.0)

    def grad_store(g, out_ref):
        def one(t, carry):
            out_ref[t] = GF[g, rows_at(t * C, C)].astype(F32)[:, 0:C] * scale
            return carry

        lax.fori_loop(0, 27, one, 0)

    start_all(plane_copies(0))
    for c in arrivals[4:7]:
        c.wait()
    GS[0:2, 0:C] = gains_ref[...]
    GS[2:4, 0:C] = shifts_ref[...]

    def load_first(t, carry):
        W1[pl.ds(pl.multiple_of(t * L, L), C), 0:C] = w1_ref[t]
        return carry

    lax.fori_loop(0, 27, load_first, 0)

    def load_rest(t, carry):
        W2[pl.ds(pl.multiple_of(t * L, L), C), 0:C] = w2_ref[t]
        whole = pl.ds(pl.multiple_of(t * L, L), L)
        back = pl.ds(pl.multiple_of((t - t % 3 + 2 - t % 3) * L, L), L)
        T1[back, :] = W1[whole, :].T
        T2[back, :] = W2[whole, :].T
        return carry

    def fill_weights():
        arrivals[7].wait()
        lax.fori_loop(0, 27, load_rest, 0)

    wait_all(plane_copies(0))
    send_faces(0, S)
    wait_all(face_copies(0))
    start_all(plane_copies(1))

    at_y = lax.broadcasted_iota(jnp.int32, (YE, L), 0)
    live_y = jnp.where(
        ((at_y == 0) & (gy == 0)) | ((at_y == YE - 1) & (gy == NGY - 1)), 0.0, 1.0
    ).astype(F32)
    live_z = [jnp.where(gz == 0, 0.0, 1.0), jnp.where(gz == NGZ - 1, 0.0, 1.0)]

    def spread_lanes(v):
        return jnp.broadcast_to(v[..., L - 1 : L], v.shape)

    def first_input(x, carry):
        gone = ((x == 0) & (gx == 0)) | ((x == XE - 1) & (gx == NGX - 1))
        live = live_y * jnp.where(gone, 0.0, 1.0)
        s = S[x]
        m = spread_lanes(s) * live[:, None, :]
        MK[x] = m
        s = s * m
        S[x] = s
        faces = []
        for k in range(2):
            f = ZR[0, k, x].astype(F32)
            mf = spread_lanes(f) * (live * live_z[k])
            MZ[k, x] = mf
            f = f * mf
            ZR[0, k, x] = f.astype(BF16)
            faces.append(f)
        put(PS, x, s, faces[0], faces[1])
        return carry

    lax.fori_loop(0, XE, first_input, 0)

    def keep_y1(h, y):
        keep(2, Y1, h, y * own(MK, h))

    convolve(PS, W1, False, keep_y1)

    def norm_begin(k, ref):
        first, count = local_sum(lambda x: (mid(ref, x), mid(MK, x)))
        mean = first / jnp.maximum(count, 1.0)

        def deviation(x):
            d = (mid(ref, x) - mean) * mid(MK, x)
            return (d * d,)

        (second,) = local_sum(deviation)
        return [first, second, count]

    def norm_exchange(k, q, ref, fill):
        rows = norm_begin(k, ref)
        sum_start(k, 0, rows)
        start_all(plane_copies(q))
        rows = sum_wait(k, 0, True)
        sum_start(k, 1, rows)
        wait_all(plane_copies(q))
        send_faces(q, ref)
        fill()
        wait_all(face_copies(q))
        rows = sum_wait(k, 1, True)
        mean = rows[0] / rows[2]
        rstd = lax.rsqrt(rows[1] / rows[2] + 1e-05)
        return mean, rstd, rows[2]

    wait_all(plane_copies(1))
    send_faces(1, CT)
    mean1, rstd1, count = norm_exchange(0, 2, Y1, fill_weights)
    gain1, gain2, shift1, shift2 = GS[0:1], GS[1:2], GS[2:3], GS[3:4]

    def second_input(x, carry):
        def act(y, m):
            n = (y - mean1) * rstd1
            pre = gain1 * n + shift1
            return n, m * (pre * sigmoid(pre))

        n, hidden = act(Y1[x], MK[x])
        N1[x] = n
        faces = []
        for k in range(2):
            nf, hf = act(ZR[2, k, x].astype(F32), MZ[k, x])
            NZ1[k, x] = nf
            faces.append(hf)
        put(PH, x, hidden, faces[0], faces[1])
        return carry

    lax.fori_loop(0, XE, second_input, 0)

    def keep_y2(h, y):
        keep(3, Y2, h, y * own(MK, h))

    convolve(PH, W2, False, keep_y2)
    spare = jnp.where(lax.broadcasted_iota(jnp.int32, (1, L), 1) == L - 1, 1.0, 0.0).astype(F32)

    def second_fill():
        wait_all(face_copies(1))
        prepare(lambda x: mid(MK, x) * (mid(N1, x) + spare))
        products(2, PS, 0, 9)
        grad_step(2, 0)

    mean2, rstd2, _ = norm_exchange(1, 3, Y2, second_fill)
    grad_step(2, 1)

    def outgoing(y, s, m, ct):
        n = (y - mean2) * rstd2
        pre = gain2 * n + shift2 + s
        sig = sigmoid(pre)
        return n, m * (pre * sig), ct * m * (sig * (1.0 + pre * (1.0 - sig)))

    lane = lax.broadcasted_iota(jnp.int32, (1, L), 1)
    inner = jnp.where(lane < C, 1.0, 0.0).astype(F32)

    def last_forward(x, carry):
        n, out, d = outgoing(Y2[x], S[x] * inner, MK[x], CT[x])
        N2[x] = n
        D2[x] = d

        @pl.when((x >= 1) & (x <= X))
        def _():
            result_ref[x - 1] = out[1 : 1 + Y, :, 0:C].astype(BF16)

        for k in range(2):
            y, s, ct = (ZR[q, k, x].astype(F32) for q in (3, 0, 1))
            nf, _, df = outgoing(y, s * inner, MZ[k, x], ct)
            NZ2[k, x] = nf
            DZ2[k, x] = df
        return carry

    lax.fori_loop(0, XE, last_forward, 0)

    results = [pltpu.make_async_copy(result_ref, result_out, outs.at[0])]
    results[0].start()

    rows = local_sum(lambda x: (mid(D2, x), mid(D2, x) * mid(N2, x)))
    sum_start(2, 0, rows)
    prepare(lambda x: mid(D2, x))
    products(1, PH, 0, 7)
    rows = sum_wait(2, 0, False)
    sum_start(2, 1, rows)
    products(1, PH, 7, 9)
    grad_step(1, 0)
    prepare(lambda x: mid(MK, x) * (mid(N2, x) + spare))
    products(3, PH, 0, 9)
    grad_step(2, 2)
    sum2, cross2 = sum_wait(2, 1, False)
    grad_step(1, 1)
    grad_step(3, 0)

    def third_input(x, carry):
        factor = gain2 * rstd2

        def back(d, n, m):
            return m * factor * (d - sum2 / count - n * cross2 / count)

        main = back(D2[x], N2[x], MK[x])
        faces = [back(DZ2[k, x], NZ2[k, x], MZ[k, x]) for k in range(2)]
        put(PD2, x, main, faces[0], faces[1])
        return carry

    lax.fori_loop(0, XE, third_input, 0)

    def keep_d1(h, v):
        pre = gain1 * own(N1, h) + shift1
        sig = sigmoid(pre)
        keep(4, D1, h, v * own(MK, h) * (sig * (1.0 + pre * (1.0 - sig))))

    convolve(PD2, T2, True, keep_d1)
    rows = local_sum(lambda x: (mid(D1, x), mid(D1, x) * mid(N1, x)))
    sum_start(3, 0, rows)
    start_all(plane_copies(4))
    grad_step(3, 1)
    prepare(lambda x: mid(D1, x))
    products(0, PS, 0, 9)
    grad_step(0, 0)
    rows = sum_wait(3, 0, False)
    sum_start(3, 1, rows)
    wait_all(plane_copies(4))
    send_faces(4, D1)
    grad_step(1, 2)
    grad_step(2, 3)
    grad_step(0, 1)
    grad_step(3, 2)
    grad_step(1, 3)
    wait_all(face_copies(4))
    sum1, cross1 = sum_wait(3, 1, False)

    def fourth_input(x, carry):
        factor = gain1 * rstd1

        def back(d, n, m):
            return m * factor * (d - sum1 / count - n * cross1 / count)

        main = back(D1[x], N1[x], MK[x])
        faces = [back(ZR[4, k, x].astype(F32), NZ1[k, x], MZ[k, x]) for k in range(2)]
        put(PD1, x, main, faces[0], faces[1])
        return carry

    lax.fori_loop(0, XE, fourth_input, 0)

    def keep_features(h, v):
        out = own(MK, h) * (own(D2, h) + v)
        gfeat_ref[pl.ds(h * H, H)] = out[:, :, :, 0:C].astype(BF16)

    convolve(PD1, T1, True, keep_features)
    at8 = lax.broadcasted_iota(jnp.int32, (8, L), 0)
    table = jnp.zeros((8, L), F32)
    for i, row in enumerate((cross1, sum1, cross2, sum2)):
        table = jnp.where(at8 == i, jnp.broadcast_to(row * scale, (8, L)), table)
    norm_ref[...] = table[0:4, 0:C]

    results.append(pltpu.make_async_copy(norm_ref, norm_out, outs.at[1]))
    results.append(pltpu.make_async_copy(gfeat_ref, gfeat_out, outs.at[2]))
    results[1].start()
    results[2].start()

    grad_step(0, 2)
    grad_step(3, 3)
    grad_step(0, 3)
    grad_step(1, 4, (sum2, cross2, gain2 * rstd2))
    grad_step(0, 4, (sum1, cross1, gain1 * rstd1))
    grad_step(1, 5)
    grad_step(0, 5)
    grad_step(1, 6)
    grad_step(0, 6)
    grad_step(1, 7)
    grad_store(1, g2_ref)
    results.append(pltpu.make_async_copy(g2_ref, g2_out, outs.at[3]))
    results[3].start()
    grad_step(0, 7)
    grad_store(0, g1_ref)
    results.append(pltpu.make_async_copy(g1_ref, g1_out, outs.at[4]))
    results[4].start()
    for c in results:
        c.wait()


def hand_over(*refs):
    ins, outs, held, (into, out) = refs[0:5], refs[5:10], refs[10:15], refs[15:17]
    first = [pltpu.make_async_copy(a, b, into.at[i]) for i, (a, b) in enumerate(zip(ins, held))]
    last = [pltpu.make_async_copy(a, b, out.at[i]) for i, (a, b) in enumerate(zip(held, outs))]
    for c in first:
        c.start()
    for a, b in zip(first, last):
        a.wait()
        b.start()
    for c in last:
        c.wait()


def local(sizes, features, ground, thickness, weight_one, weight_two, gains, shifts, cotangent):
    NGX, NGY, NGZ = sizes
    X, Y, Z, C = features.shape
    n_y, n_z = NGZ // 2, NGX
    n = (n_y, n_z, NGY)
    pairs = [n[p] * n[(p + 1) % 3] for p in range(3)]
    tiles = -(-27 * C // (2 * 16 * min(pairs)))
    segs = tuple(16 * (tiles // 3 + (p < tiles % 3)) for p in range(3))
    dims = (NGX, NGY, NGZ, X, Y, Z, C, segs)
    XE, YE = X + 2, Y + 2
    ext = pltpu.VMEM((XE, YE, Z, L), F32)
    face = pltpu.VMEM((2, XE, YE, L), F32)
    patch = pltpu.VMEM((XE, YE, Z, 3 * L), BF16)
    weights = pltpu.VMEM((27 * L, L), BF16)
    dma = pltpu.SemaphoreType.DMA
    scratch = [
        pltpu.VMEM((X, Y, Z, C), BF16),
        pltpu.VMEM((X, Y, Z, C), BF16),
        pltpu.VMEM((27, C, C), BF16),
        pltpu.VMEM((27, C, C), BF16),
        pltpu.VMEM((2, C), F32),
        pltpu.VMEM((2, C), F32),
        pltpu.SMEM((X, Y), jnp.int32),
        pltpu.SMEM((X, Y), jnp.int32),
        pltpu.VMEM((X, Y, Z, C), BF16),
        pltpu.VMEM((X, Y, Z, C), BF16),
        pltpu.VMEM((27, C, C), F32),
        pltpu.VMEM((27, C, C), F32),
        pltpu.VMEM((4, C), F32),
    ]
    scratch += [pltpu.VMEM((5, XE, YE, Z, L), BF16)]
    scratch += [ext] * 9
    scratch += [pltpu.VMEM((5, 2, XE, YE, L), BF16)] * 2
    scratch += [face] * 4
    scratch += [pltpu.VMEM((YE, Z + 16, L), F32)]
    scratch += [patch] * 4
    scratch += [pltpu.VMEM((L, X * Y * Z), BF16)]
    scratch += [weights] * 4
    scratch += [pltpu.VMEM((8, L), F32)]
    n_a, n_b = 2 * n_z, NGY * n_y
    scratch += [pltpu.VMEM((4, 2, 4, L), F32)]
    scratch += [pltpu.VMEM((4, k, 4, L), F32) for k in (n_a, n_b)]
    len_c = sum(a * b for a, b in zip(pairs, segs))
    scratch += [
        pltpu.VMEM((4, 2 * len_c, L), F32),
        pltpu.VMEM((4, len_c, L), F32),
        pltpu.VMEM((2, 2 * len_c, L), BF16),
    ]
    for p in range(3):
        n1, n2, n3 = n[p], n[(p + 1) % 3], n[(p + 2) % 3]
        seg = segs[p]
        scratch += [
            pltpu.VMEM((4, n1 * n2 * seg, L), F32),
            pltpu.VMEM((4, n1 - 1, n2 * seg, L), F32),
            pltpu.VMEM((4, n2 * seg, L), F32),
            pltpu.VMEM((4, n2 - 1, seg, L), F32),
            pltpu.VMEM((4, seg, L), F32),
            pltpu.VMEM((4, n3, seg, L), F32),
        ]
    most = max(n) - 1
    scratch += [dma((5, 8)), dma((5, 8)), dma((5, 2)), dma((5, 2))]
    scratch += [dma((n_a + n_b,)), dma((4, n_a + n_b))]
    scratch += [dma((4, 3 * most)), dma((22, 3 * most))]
    scratch += [dma((8,)), dma((5,))]
    anywhere = pl.BlockSpec(memory_space=pl.ANY)
    shapes = (
        jax.ShapeDtypeStruct((X, Y, Z, C), BF16),
        jax.ShapeDtypeStruct((X, Y, Z, C), BF16),
        jax.ShapeDtypeStruct((27, C, C), F32),
        jax.ShapeDtypeStruct((27, C, C), F32),
        jax.ShapeDtypeStruct((4, C), F32),
    )
    outs = pl.pallas_call(
        functools.partial(body, dims),
        out_shape=shapes,
        in_specs=[pl.BlockSpec(memory_space=pltpu.HBM)] * 8,
        out_specs=(anywhere,) * 5,
        scratch_shapes=scratch,
        compiler_params=pltpu.CompilerParams(
            collective_id=0, has_side_effects=True, vmem_limit_bytes=VMEM_BYTES
        ),
    )(features, ground, thickness, weight_one, weight_two, gains, shifts, cotangent)
    return pl.pallas_call(
        hand_over,
        out_shape=shapes,
        in_specs=[anywhere] * 5,
        out_specs=(pl.BlockSpec(memory_space=pltpu.HBM),) * 5,
        scratch_shapes=[pltpu.VMEM(v.shape, v.dtype) for v in shapes] + [dma((5,)), dma((5,))],
        compiler_params=pltpu.CompilerParams(vmem_limit_bytes=VMEM_BYTES),
    )(*outs)


def solution(mesh):
    sizes = tuple(mesh.shape[a] for a in ("gx", "gy", "gz"))
    return jax.shard_map(
        functools.partial(local, sizes),
        mesh=mesh,
        in_specs=(
            P("gx", "gy", "gz", None),
            P("gx", "gy"),
            P("gx", "gy"),
            P(),
            P(),
            P(),
            P(),
            P("gx", "gy", "gz", None),
        ),
        out_specs=(P("gx", "gy", "gz", None), P("gx", "gy", "gz", None), P(), P(), P()),
        check_vma=False,
    )
```

```python
import functools
import math

import jax
import jax.numpy as jnp
from jax import lax
from jax.experimental import pallas as pl
from jax.experimental.pallas import tpu as pltpu
from jax.sharding import PartitionSpec as P

MESH = pl.DeviceIdType.MESH
F32 = jnp.float32
BF16 = jnp.bfloat16
L = 128
VMEM_BYTES = 63400000
SIDES = [(dx, dy) for dx in (-1, 0, 1) for dy in (-1, 0, 1) if (dx, dy) != (0, 0)]
FACES = [(k, dx, dy) for k in (0, 1) for dx in (-1, 0, 1) for dy in (-1, 0, 1)]


def sigmoid(v):
    return 1.0 / (1.0 + jnp.exp(-v))


def body(
    dims,
    feat_in, ground_in, thick_in, w1_in, w2_in, gains_in, shifts_in, cot_in,
    result_out, gfeat_out, g1_out, g2_out, norm_out,
    feat_ref, cot_ref, w1_ref, w2_ref, gains_ref, shifts_ref, ground_ref, thick_ref,
    result_ref, gfeat_ref, g1_ref, g2_ref, norm_ref,
    HB, S, CT, Y1, Y2, D1, MK, N1, N2, D2,
    ZC, ZY, RC, RX, RY, RK, ZE, MZ, NZ1, NZ2, DZ2,
    V, PS, PH, PD2, PD1, DT, W1, W2, T1, T2, GS,
    STS, RA, RB,
    GA, GC, GF, *rest,
):
    NGX, NGY, NGZ, X, Y, Z, C, segs = dims
    portions = [rest[6 * p : 6 * p + 6] for p in range(3)]
    hs, hr, zs, zr, ss, sr, gs, gr, ins, outs = rest[18:]
    XE, YE = X + 2, Y + 2
    gx, gy, gz = lax.axis_index("gx"), lax.axis_index("gy"), lax.axis_index("gz")
    nz_lo, n_y = NGX // 2, NGZ // 2
    core, z_lo = gx % 2, gx // 2
    row_y, z_hi = gz // 2, gz % 2
    n_z = nz_lo * 2
    pos_z = z_hi * nz_lo + z_lo

    def dev(ax, ay, az):
        return (ax, ay, az)

    def peer_y(j):
        return dev(gx, (gy + j) % NGY, gz)

    def side(dx, dy):
        return dev((gx + dx + NGX) % NGX, (gy + dy + NGY) % NGY, gz)

    def grad_y(j):
        return dev(gx, gy, ((row_y + j) % n_y) * 2 + z_hi)

    def grad_z(j):
        other = (pos_z + j) % n_z
        return dev((other % nz_lo) * 2 + core, gy, row_y * 2 + other // nz_lo)

    partner = dev(z_lo * 2 + 1 - core, gy, gz)
    n_a, n_b = 2 * n_z, NGY * n_y
    me_a, me_b = pos_z * 2 + core, gy * n_y + row_y

    def peer_a(j):
        other = (me_a + j) % n_a
        pos = other // 2
        return dev((pos % nz_lo) * 2 + other % 2, gy, row_y * 2 + pos // nz_lo)

    def peer_b(j):
        other = (me_b + j) % n_b
        return dev(gx, other // n_y, (other % n_y) * 2 + z_hi)

    def beyond(k, dx, dy):
        z = (gz + NGZ - 1) % NGZ if k == 0 else (gz + 1) % NGZ
        return dev((gx + dx + NGX) % NGX, (gy + dy + NGY) % NGY, z)


    greet = [peer_a(j) for j in range(1, n_a)]
    greet += [peer_b(j) for j in range(1, n_b)]
    greet += [beyond(k, dx, dy) for k, dx, dy in FACES]
    greet += [side(dx, dy) for dx, dy in SIDES]
    barrier = pltpu.get_barrier_semaphore()
    for other in greet:
        pl.semaphore_signal(barrier, inc=1, device_id=other, device_id_type=MESH)

    arrivals = [
        pltpu.make_async_copy(src, dst, ins.at[i])
        for i, (src, dst) in enumerate(
            (
                (ground_in, ground_ref), (thick_in, thick_ref), (feat_in, feat_ref),
                (cot_in, cot_ref), (w1_in, w1_ref), (gains_in, gains_ref),
                (shifts_in, shifts_ref), (w2_in, w2_ref),
            )
        )
    ]
    for c in arrivals:
        c.start()

    for ref in (W1, W2, T1, T2, GS):
        ref[...] = jnp.zeros(ref.shape, ref.dtype)
    for c in arrivals[:4]:
        c.wait()

    def load_block(x, carry):
        level = lax.broadcasted_iota(jnp.int32, (Z, L), 0) + gz * Z
        for y in range(Y):
            low = ground_ref[x, y]
            high = low + thick_ref[x, y]
            m = jnp.where((level >= low) & (level < high), 1.0, 0.0).astype(F32)
            S[1 + x, 1 + y] = m
            S[1 + x, 1 + y, :, 0:C] = m[:, 0:C] * feat_ref[x, y].astype(F32)
            CT[1 + x, 1 + y] = jnp.zeros((Z, L), F32)
            CT[1 + x, 1 + y, :, 0:C] = cot_ref[x, y].astype(F32)
            HB[0, 1 + x, 1 + y] = S[1 + x, 1 + y].astype(BF16)
            HB[1, 1 + x, 1 + y] = CT[1 + x, 1 + y].astype(BF16)
        return carry

    lax.fori_loop(0, X, load_block, 0)
    pl.semaphore_wait(barrier, len(greet))

    def cut(d, n, sending):
        if d == 0:
            return pl.ds(1, n)
        if sending:
            return pl.ds(n if d > 0 else 1, 1)
        return pl.ds(0 if d > 0 else n + 1, 1)

    def plane_copies(q):
        out = []
        for k, (dx, dy) in enumerate(SIDES):
            out.append(
                pltpu.make_async_remote_copy(
                    src_ref=HB.at[q, cut(dx, X, True), cut(dy, Y, True)],
                    dst_ref=HB.at[q, cut(dx, X, False), cut(dy, Y, False)],
                    send_sem=hs.at[q, k],
                    recv_sem=hr.at[q, k],
                    device_id=side(dx, dy),
                    device_id_type=MESH,
                )
            )
        return out

    def face_copies(q):
        out = []
        for i, (k, dx, dy) in enumerate(FACES):
            edge_x, side_x = (X - 1, 0) if dx > 0 else (0, 1)
            edge_y, side_y = (1, 0) if dy > 0 else (0, 1)
            if dx and dy:
                src, dst = ZC.at[q, k, edge_x], RK.at[q, 1 - k, side_x, side_y]
            elif dx:
                src, dst = ZC.at[q, k, edge_x], RX.at[q, 1 - k, side_x]
            elif dy:
                src, dst = ZY.at[q, k, edge_y], RY.at[q, 1 - k, side_y]
            else:
                src, dst = ZC.at[q, k], RC.at[q, 1 - k]
            out.append(
                pltpu.make_async_remote_copy(
                    src_ref=src,
                    dst_ref=dst,
                    send_sem=zs.at[int(q == 1), i],
                    recv_sem=zr.at[q, i],
                    device_id=beyond(k, dx, dy),
                    device_id_type=MESH,
                )
            )
        return out

    def start_all(copies):
        for c in copies:
            c.start()

    def wait_all(copies):
        for c in copies:
            c.wait()

    def halo_start(q, ref):
        def one(x, carry):
            for k, z in ((0, 0), (1, Z - 1)):
                ZC[q, k, x] = ref[1 + x, 1 : 1 + Y, z, :].astype(BF16)
            return carry

        start_all(plane_copies(q))
        lax.fori_loop(0, X, one, 0)
        for k, z in ((0, 0), (1, Z - 1)):
            for i, y in ((0, 1), (1, Y)):
                ZY[q, k, i] = ref[1 : 1 + X, y, z, :].astype(BF16)
        start_all(face_copies(q))

    def halo_finish(q, ref):
        wait_all(plane_copies(q))
        wait_all(face_copies(q))
        if q > 1:
            for at in (0, XE - 1):
                ref[at] = HB[q, at].astype(F32)
            for at in (0, YE - 1):
                ref[1 : 1 + X, at] = HB[q, 1 : 1 + X, at].astype(F32)
        for k in range(2):
            def one(x, carry):
                ZE[q, k, 1 + x, 1 : 1 + Y] = RC[q, k, x].astype(F32)
                return carry

            lax.fori_loop(0, X, one, 0)
            for i, at_x in ((0, 0), (1, XE - 1)):
                ZE[q, k, at_x, 1 : 1 + Y] = RX[q, k, i].astype(F32)
                for j, at_y in ((0, 0), (1, YE - 1)):
                    row = Y - 1 if j == 0 else 0
                    tile = RK[q, k, i, j].astype(F32)
                    ZE[q, k, at_x, at_y : at_y + 1] = tile[row : row + 1]
            for j, at_y in ((0, 0), (1, YE - 1)):
                tile = RY[q, k, j].astype(F32)
                for x in range(X):
                    ZE[q, k, 1 + x, at_y : at_y + 1] = tile[x : x + 1]

    def sum_copies(k, part):
        n, me, peer, land = ((n_a, me_a, peer_a, RA), (n_b, me_b, peer_b, RB))[part]
        base = (0, n_a)[part]
        return [
            pltpu.make_async_remote_copy(
                src_ref=STS.at[k, part],
                dst_ref=land.at[k, me],
                send_sem=ss.at[base + j],
                recv_sem=sr.at[k, base + j],
                device_id=peer(j),
                device_id_type=MESH,
            )
            for j in range(1, n)
        ]

    def sum_start(k, part, rows):
        at = lax.broadcasted_iota(jnp.int32, (4, L), 0)
        tile = jnp.zeros((4, L), F32)
        for i, row in enumerate(rows):
            tile = jnp.where(at == i, jnp.broadcast_to(row, (4, L)), tile)
        STS[k, part] = tile
        me, land = ((me_a, RA), (me_b, RB))[part]
        land[k, me] = tile
        start_all(sum_copies(k, part))

    def sum_wait(k, part, spread):
        n, land = ((n_a, RA), (n_b, RB))[part]
        wait_all(sum_copies(k, part))
        tiles = land[k]
        first, second, third = (jnp.sum(tiles[:, i], axis=0, keepdims=True) for i in range(3))
        if not spread:
            return [first, second]
        mean = first / jnp.maximum(third, 1.0)
        each = tiles[:, 0] / jnp.maximum(tiles[:, 2], 1.0) - mean
        second = second + jnp.sum(tiles[:, 2] * each * each, axis=0, keepdims=True)
        return [first, second, third]

    def put(dest, x, main, low, high):
        V[:, 8 : 8 + Z, :] = main
        for y in range(YE):
            V[y, 7:8, :] = low[y : y + 1]
            V[y, 8 + Z : 9 + Z, :] = high[y : y + 1]
        for c in range(3):
            dest[x, :, :, c * L : (c + 1) * L] = V[:, 7 + c : 7 + c + Z, :].astype(BF16)

    H = X // 2

    def convolve(src, weights, flipped, finish):
        def half(h, carry):
            total = None
            for k0 in range(0, 9, 2):
                parts = []
                for k in range(k0, min(k0 + 2, 9)):
                    a, b = k // 3, k % 3
                    if flipped:
                        a, b = 2 - a, 2 - b
                    parts.append(
                        src[pl.ds(h * H + a, H), b : b + Y, :, :].reshape(H * Y * Z, 3 * L)
                    )
                left = jnp.concatenate(parts, axis=1) if len(parts) > 1 else parts[0]
                right = weights[k0 * 3 * L : (k0 * 3 + 3 * len(parts)) * L, :]
                term = jnp.dot(left, right, preferred_element_type=F32)
                total = term if total is None else total + term
            finish(h, total.reshape(H, Y, Z, L))
            return carry

        lax.fori_loop(0, 2, half, 0)

    def own(ref, h):
        return ref[pl.ds(1 + h * H, H), 1 : 1 + Y, :, :]

    def keep(q, ref, h, v):
        ref[pl.ds(1 + h * H, H), 1 : 1 + Y, :, :] = v
        HB[q, pl.ds(1 + h * H, H), 1 : 1 + Y, :, :] = v.astype(BF16)

    def local_sum(terms):
        def one(x, carry):
            return tuple(c + jnp.sum(t, axis=0) for c, t in zip(carry, terms(1 + x)))

        zero = tuple(jnp.zeros((Z, L), F32) for _ in terms(1))
        out = lax.fori_loop(0, X, one, zero)
        return [jnp.sum(v, axis=0, keepdims=True) for v in out]

    def mid(ref, x):
        return ref[x, 1 : 1 + Y, :, :]

    def prepare(get):
        for x in range(X):
            DT[:, x * Y * Z : (x + 1) * Y * Z] = get(1 + x).reshape(Y * Z, L).astype(BF16).T

    def products(g, src, first, last):
        def one(k, carry):
            a, b = k // 3, k % 3
            patch = src[pl.ds(a, X), pl.ds(b, Y), :, :].reshape(X * Y * Z, 3 * L)
            out = jnp.dot(DT[...], patch, preferred_element_type=F32)
            for c in range(3):
                GA[g, pl.ds(pl.multiple_of((3 * k + c) * C, 16), C), :] = (
                    out[:, c * L : (c + 1) * L].T[0:C]
                )
            return carry

        lax.fori_loop(first, last, one, 0)

    axes = ((n_y, row_y, grad_y), (n_z, pos_z, grad_z), (NGY, gy, peer_y))
    plans = []
    base = 0
    for p in range(3):
        plan = [axes[(p + i) % 3] for i in range(3)]
        len1 = plan[1][0] * segs[p]
        plans.append((plan, base, len1, segs[p]))
        base += plan[0][0] * len1
    len_c = base

    def rows_at(off, n):
        return pl.ds(pl.multiple_of(off, 16), n)

    most = max(n_y, n_z, NGY) - 1

    def grad_copies(g, stage):
        def copy(src, dst, k, other):
            return pltpu.make_async_remote_copy(
                src_ref=src, dst_ref=dst, send_sem=gs.at[g, k],
                recv_sem=gr.at[g * 7 + stage if g < 2 else 6 + g * 4 + stage, k], device_id=other, device_id_type=MESH,
            )

        if stage == 0:
            return [copy(GA.at[g, rows_at((1 - core) * len_c, len_c)], GC.at[g], 0, partner)]
        if stage == 6:
            part = GF.at[g, rows_at(core * len_c, len_c)]
            return [copy(part, part, 0, partner)]
        out = []
        for p, (plan, base, len1, seg) in enumerate(plans):
            GB, GY, GD, GZ, GE, GX = portions[p]
            n, me, peer = plan[(None, 0, 1, 2, 1, 0)[stage]]
            off1 = core * len_c + base + plan[0][1] * len1
            off2 = off1 + plan[1][1] * seg
            for j in range(1, n):
                if stage == 1:
                    part = GB.at[g, rows_at(((me + j) % n) * len1, len1)]
                    land = GY.at[g, j - 1]
                elif stage == 2:
                    part = GD.at[g, rows_at(((me + j) % n) * seg, seg)]
                    land = GZ.at[g, j - 1]
                elif stage == 3:
                    part, land = GE.at[g], GX.at[g, me]
                elif stage == 4:
                    part = land = GF.at[g, rows_at(off2, seg)]
                else:
                    part = land = GF.at[g, rows_at(off1, len1)]
                out.append(copy(part, land, p * most + j - 1, peer(j)))
        return out

    def grad_step(g, stage, late=None):
        if stage > 0:
            wait_all(grad_copies(g, stage - 1))
        if stage == 4:
            wait_all(grad_copies(g + 2, 3))
        for p, (plan, base, len1, seg) in enumerate(plans):
            GB, GY, GD, GZ, GE, GX = portions[p]
            if stage == 1:
                def fold(i, carry):
                    at = i * len1 + base
                    GB[g, rows_at(i * len1, len1)] = (
                        GA[g, rows_at(core * len_c + at, len1)] + GC[g, rows_at(at, len1)]
                    )
                    return carry

                lax.fori_loop(0, plan[0][0], fold, 0)
            if stage == 2:
                v = GB[g, rows_at(plan[0][1] * len1, len1)]
                for j in range(plan[0][0] - 1):
                    v = v + GY[g, j]
                GD[g] = v
            if stage == 3:
                v = GD[g, rows_at(plan[1][1] * seg, seg)]
                for j in range(plan[1][0] - 1):
                    v = v + GZ[g, j]
                GE[g] = v
                GX[g, plan[2][1]] = v
            if stage == 4:
                v, w = GX[g, 0], GX[g + 2, 0]
                for j in range(1, plan[2][0]):
                    v = v + GX[g, j]
                    w = w + GX[g + 2, j]
                total, cross, factor = late
                v = factor * (v - (total / count) * spread_lanes(w) - (cross / count) * w)
                off = core * len_c + base + plan[0][1] * len1 + plan[1][1] * seg
                GF[g, rows_at(off, seg)] = v.astype(BF16)
        if stage < 7:
            start_all(grad_copies(g, stage))

    total_cells = X * NGX * Y * NGY * Z * NGZ
    scale = 1.0 / math.sqrt(total_cells / 8.0)

    def grad_store(g, out_ref):
        def one(t, carry):
            out_ref[t] = GF[g, rows_at(t * C, C)].astype(F32)[:, 0:C] * scale
            return carry

        lax.fori_loop(0, 27, one, 0)

    halo_start(0, S)
    for c in arrivals[4:7]:
        c.wait()
    GS[0:2, 0:C] = gains_ref[...]
    GS[2:4, 0:C] = shifts_ref[...]

    def load_first(t, carry):
        W1[pl.ds(pl.multiple_of(t * L, L), C), 0:C] = w1_ref[t]
        return carry

    lax.fori_loop(0, 27, load_first, 0)

    def load_rest(t, carry):
        W2[pl.ds(pl.multiple_of(t * L, L), C), 0:C] = w2_ref[t]
        whole = pl.ds(pl.multiple_of(t * L, L), L)
        back = pl.ds(pl.multiple_of((t - t % 3 + 2 - t % 3) * L, L), L)
        T1[back, :] = W1[whole, :].T
        T2[back, :] = W2[whole, :].T
        return carry

    def fill_weights():
        arrivals[7].wait()
        lax.fori_loop(0, 27, load_rest, 0)

    halo_finish(0, S)
    halo_start(1, CT)

    at_y = lax.broadcasted_iota(jnp.int32, (YE, L), 0)
    live_y = jnp.where(
        ((at_y == 0) & (gy == 0)) | ((at_y == YE - 1) & (gy == NGY - 1)), 0.0, 1.0
    ).astype(F32)
    live_z = [jnp.where(gz == 0, 0.0, 1.0), jnp.where(gz == NGZ - 1, 0.0, 1.0)]

    def spread_lanes(v):
        return jnp.broadcast_to(v[..., L - 1 : L], v.shape)

    def first_input(x, carry):
        gone = ((x == 0) & (gx == 0)) | ((x == XE - 1) & (gx == NGX - 1))
        live = live_y * jnp.where(gone, 0.0, 1.0)
        s = HB[0, x].astype(F32)
        m = spread_lanes(s) * live[:, None, :]
        MK[x] = m
        s = s * m
        S[x] = s
        faces = []
        for k in range(2):
            f = ZE[0, k, x]
            mf = spread_lanes(f) * (live * live_z[k])
            MZ[k, x] = mf
            f = f * mf
            ZE[0, k, x] = f
            faces.append(f)
        put(PS, x, s, faces[0], faces[1])
        return carry

    lax.fori_loop(0, XE, first_input, 0)

    def keep_y1(h, y):
        keep(2, Y1, h, y * own(MK, h))

    convolve(PS, W1, False, keep_y1)

    def norm_begin(k, ref):
        first, count = local_sum(lambda x: (mid(ref, x), mid(MK, x)))
        mean = first / jnp.maximum(count, 1.0)

        def deviation(x):
            d = (mid(ref, x) - mean) * mid(MK, x)
            return (d * d,)

        (second,) = local_sum(deviation)
        return [first, second, count]

    def norm_exchange(k, q, ref, fill):
        rows = norm_begin(k, ref)
        sum_start(k, 0, rows)
        halo_start(q, ref)
        rows = sum_wait(k, 0, True)
        sum_start(k, 1, rows)
        fill()
        halo_finish(q, ref)
        rows = sum_wait(k, 1, True)
        mean = rows[0] / rows[2]
        rstd = lax.rsqrt(rows[1] / rows[2] + 1e-05)
        return mean, rstd, rows[2]

    mean1, rstd1, count = norm_exchange(0, 2, Y1, fill_weights)
    gain1, gain2, shift1, shift2 = GS[0:1], GS[1:2], GS[2:3], GS[3:4]

    def second_input(x, carry):
        def act(y, m):
            n = (y - mean1) * rstd1
            pre = gain1 * n + shift1
            return n, m * (pre * sigmoid(pre))

        n, hidden = act(Y1[x], MK[x])
        N1[x] = n
        faces = []
        for k in range(2):
            nf, hf = act(ZE[2, k, x], MZ[k, x])
            NZ1[k, x] = nf
            faces.append(hf)
        put(PH, x, hidden, faces[0], faces[1])
        return carry

    lax.fori_loop(0, XE, second_input, 0)

    def keep_y2(h, y):
        keep(3, Y2, h, y * own(MK, h))

    convolve(PH, W2, False, keep_y2)
    spare = jnp.where(lax.broadcasted_iota(jnp.int32, (1, L), 1) == L - 1, 1.0, 0.0).astype(F32)

    def second_fill():
        halo_finish(1, CT)
        prepare(lambda x: mid(MK, x) * (mid(N1, x) + spare))
        products(2, PS, 0, 9)
        grad_step(2, 0)

    mean2, rstd2, _ = norm_exchange(1, 3, Y2, second_fill)

    def outgoing(y, s, m, ct):
        n = (y - mean2) * rstd2
        pre = gain2 * n + shift2 + s
        sig = sigmoid(pre)
        return n, m * (pre * sig), ct * m * (sig * (1.0 + pre * (1.0 - sig)))

    lane = lax.broadcasted_iota(jnp.int32, (1, L), 1)
    inner = jnp.where(lane < C, 1.0, 0.0).astype(F32)

    def last_forward(x, carry):
        n, out, d = outgoing(Y2[x], S[x] * inner, MK[x], HB[1, x].astype(F32))
        N2[x] = n
        D2[x] = d

        @pl.when((x >= 1) & (x <= X))
        def _():
            result_ref[x - 1] = out[1 : 1 + Y, :, 0:C].astype(BF16)

        for k in range(2):
            y, s, ct = (ZE[q, k, x] for q in (3, 0, 1))
            nf, _, df = outgoing(y, s * inner, MZ[k, x], ct)
            NZ2[k, x] = nf
            DZ2[k, x] = df
        return carry

    lax.fori_loop(0, XE, last_forward, 0)

    results = [pltpu.make_async_copy(result_ref, result_out, outs.at[0])]
    results[0].start()

    rows = local_sum(lambda x: (mid(D2, x), mid(D2, x) * mid(N2, x)))
    sum_start(2, 0, rows)
    grad_step(2, 1)
    prepare(lambda x: mid(D2, x))
    products(1, PH, 0, 7)
    rows = sum_wait(2, 0, False)
    sum_start(2, 1, rows)
    products(1, PH, 7, 9)
    grad_step(1, 0)
    prepare(lambda x: mid(MK, x) * (mid(N2, x) + spare))
    products(3, PH, 0, 9)
    grad_step(2, 2)
    sum2, cross2 = sum_wait(2, 1, False)
    grad_step(1, 1)
    grad_step(3, 0)

    def third_input(x, carry):
        factor = gain2 * rstd2

        def back(d, n, m):
            return m * factor * (d - sum2 / count - n * cross2 / count)

        main = back(D2[x], N2[x], MK[x])
        faces = [back(DZ2[k, x], NZ2[k, x], MZ[k, x]) for k in range(2)]
        put(PD2, x, main, faces[0], faces[1])
        return carry

    lax.fori_loop(0, XE, third_input, 0)

    def keep_d1(h, v):
        pre = gain1 * own(N1, h) + shift1
        sig = sigmoid(pre)
        keep(4, D1, h, v * own(MK, h) * (sig * (1.0 + pre * (1.0 - sig))))

    convolve(PD2, T2, True, keep_d1)
    rows = local_sum(lambda x: (mid(D1, x), mid(D1, x) * mid(N1, x)))
    sum_start(3, 0, rows)
    halo_start(4, D1)
    grad_step(3, 1)
    prepare(lambda x: mid(D1, x))
    products(0, PS, 0, 9)
    grad_step(0, 0)
    rows = sum_wait(3, 0, False)
    sum_start(3, 1, rows)
    grad_step(1, 2)
    grad_step(2, 3)
    grad_step(0, 1)
    grad_step(3, 2)
    grad_step(1, 3)
    halo_finish(4, D1)
    sum1, cross1 = sum_wait(3, 1, False)

    def fourth_input(x, carry):
        factor = gain1 * rstd1

        def back(d, n, m):
            return m * factor * (d - sum1 / count - n * cross1 / count)

        main = back(D1[x], N1[x], MK[x])
        faces = [back(ZE[4, k, x], NZ1[k, x], MZ[k, x]) for k in range(2)]
        put(PD1, x, main, faces[0], faces[1])
        return carry

    lax.fori_loop(0, XE, fourth_input, 0)

    def keep_features(h, v):
        out = own(MK, h) * (own(D2, h) + v)
        gfeat_ref[pl.ds(h * H, H)] = out[:, :, :, 0:C].astype(BF16)

    convolve(PD1, T1, True, keep_features)
    at8 = lax.broadcasted_iota(jnp.int32, (8, L), 0)
    table = jnp.zeros((8, L), F32)
    for i, row in enumerate((cross1, sum1, cross2, sum2)):
        table = jnp.where(at8 == i, jnp.broadcast_to(row * scale, (8, L)), table)
    norm_ref[...] = table[0:4, 0:C]

    results.append(pltpu.make_async_copy(norm_ref, norm_out, outs.at[1]))
    results.append(pltpu.make_async_copy(gfeat_ref, gfeat_out, outs.at[2]))
    results[1].start()
    results[2].start()

    grad_step(0, 2)
    grad_step(3, 3)
    grad_step(0, 3)
    grad_step(1, 4, (sum2, cross2, gain2 * rstd2))
    grad_step(0, 4, (sum1, cross1, gain1 * rstd1))
    grad_step(1, 5)
    grad_step(0, 5)
    grad_step(1, 6)
    grad_step(0, 6)
    grad_step(1, 7)
    grad_store(1, g2_ref)
    results.append(pltpu.make_async_copy(g2_ref, g2_out, outs.at[3]))
    results[3].start()
    grad_step(0, 7)
    grad_store(0, g1_ref)
    results.append(pltpu.make_async_copy(g1_ref, g1_out, outs.at[4]))
    results[4].start()
    for c in results:
        c.wait()


def hand_over(*refs):
    ins, outs, held, (into, out) = refs[0:5], refs[5:10], refs[10:15], refs[15:17]
    first = [pltpu.make_async_copy(a, b, into.at[i]) for i, (a, b) in enumerate(zip(ins, held))]
    last = [pltpu.make_async_copy(a, b, out.at[i]) for i, (a, b) in enumerate(zip(held, outs))]
    for c in first:
        c.start()
    for a, b in zip(first, last):
        a.wait()
        b.start()
    for c in last:
        c.wait()


def local(sizes, features, ground, thickness, weight_one, weight_two, gains, shifts, cotangent):
    NGX, NGY, NGZ = sizes
    X, Y, Z, C = features.shape
    n_y, n_z = NGZ // 2, NGX
    n = (n_y, n_z, NGY)
    pairs = [n[p] * n[(p + 1) % 3] for p in range(3)]
    tiles = -(-27 * C // (2 * 16 * min(pairs)))
    segs = tuple(16 * (tiles // 3 + (p < tiles % 3)) for p in range(3))
    dims = (NGX, NGY, NGZ, X, Y, Z, C, segs)
    XE, YE = X + 2, Y + 2
    ext = pltpu.VMEM((XE, YE, Z, L), F32)
    face = pltpu.VMEM((2, XE, YE, L), F32)
    patch = pltpu.VMEM((XE, YE, Z, 3 * L), BF16)
    weights = pltpu.VMEM((27 * L, L), BF16)
    dma = pltpu.SemaphoreType.DMA
    scratch = [
        pltpu.VMEM((X, Y, Z, C), BF16),
        pltpu.VMEM((X, Y, Z, C), BF16),
        pltpu.VMEM((27, C, C), BF16),
        pltpu.VMEM((27, C, C), BF16),
        pltpu.VMEM((2, C), F32),
        pltpu.VMEM((2, C), F32),
        pltpu.SMEM((X, Y), jnp.int32),
        pltpu.SMEM((X, Y), jnp.int32),
        pltpu.VMEM((X, Y, Z, C), BF16),
        pltpu.VMEM((X, Y, Z, C), BF16),
        pltpu.VMEM((27, C, C), F32),
        pltpu.VMEM((27, C, C), F32),
        pltpu.VMEM((4, C), F32),
    ]
    scratch += [pltpu.VMEM((5, XE, YE, Z, L), BF16)]
    scratch += [ext] * 9
    scratch += [
        pltpu.VMEM((5, 2, X, Y, L), BF16),
        pltpu.VMEM((5, 2, 2, X, L), BF16),
        pltpu.VMEM((5, 2, X, Y, L), BF16),
        pltpu.VMEM((5, 2, 2, Y, L), BF16),
        pltpu.VMEM((5, 2, 2, X, L), BF16),
        pltpu.VMEM((5, 2, 2, 2, Y, L), BF16),
        pltpu.VMEM((5, 2, XE, YE, L), F32),
    ]
    scratch += [face] * 4
    scratch += [pltpu.VMEM((YE, Z + 16, L), F32)]
    scratch += [patch] * 4
    scratch += [pltpu.VMEM((L, X * Y * Z), BF16)]
    scratch += [weights] * 4
    scratch += [pltpu.VMEM((8, L), F32)]
    n_a, n_b = 2 * n_z, NGY * n_y
    scratch += [pltpu.VMEM((4, 2, 4, L), F32)]
    scratch += [pltpu.VMEM((4, k, 4, L), F32) for k in (n_a, n_b)]
    len_c = sum(a * b for a, b in zip(pairs, segs))
    scratch += [
        pltpu.VMEM((4, 2 * len_c, L), F32),
        pltpu.VMEM((4, len_c, L), F32),
        pltpu.VMEM((2, 2 * len_c, L), BF16),
    ]
    for p in range(3):
        n1, n2, n3 = n[p], n[(p + 1) % 3], n[(p + 2) % 3]
        seg = segs[p]
        scratch += [
            pltpu.VMEM((4, n1 * n2 * seg, L), F32),
            pltpu.VMEM((4, n1 - 1, n2 * seg, L), F32),
            pltpu.VMEM((4, n2 * seg, L), F32),
            pltpu.VMEM((4, n2 - 1, seg, L), F32),
            pltpu.VMEM((4, seg, L), F32),
            pltpu.VMEM((4, n3, seg, L), F32),
        ]
    most = max(n) - 1
    scratch += [dma((5, 8)), dma((5, 8)), dma((2, 18)), dma((5, 18))]
    scratch += [dma((n_a + n_b,)), dma((4, n_a + n_b))]
    scratch += [dma((4, 3 * most)), dma((22, 3 * most))]
    scratch += [dma((8,)), dma((5,))]
    anywhere = pl.BlockSpec(memory_space=pl.ANY)
    shapes = (
        jax.ShapeDtypeStruct((X, Y, Z, C), BF16),
        jax.ShapeDtypeStruct((X, Y, Z, C), BF16),
        jax.ShapeDtypeStruct((27, C, C), F32),
        jax.ShapeDtypeStruct((27, C, C), F32),
        jax.ShapeDtypeStruct((4, C), F32),
    )
    outs = pl.pallas_call(
        functools.partial(body, dims),
        out_shape=shapes,
        in_specs=[pl.BlockSpec(memory_space=pltpu.HBM)] * 8,
        out_specs=(anywhere,) * 5,
        scratch_shapes=scratch,
        compiler_params=pltpu.CompilerParams(
            collective_id=0, has_side_effects=True, vmem_limit_bytes=VMEM_BYTES
        ),
    )(features, ground, thickness, weight_one, weight_two, gains, shifts, cotangent)
    return pl.pallas_call(
        hand_over,
        out_shape=shapes,
        in_specs=[anywhere] * 5,
        out_specs=(pl.BlockSpec(memory_space=pltpu.HBM),) * 5,
        scratch_shapes=[pltpu.VMEM(v.shape, v.dtype) for v in shapes] + [dma((5,)), dma((5,))],
        compiler_params=pltpu.CompilerParams(vmem_limit_bytes=VMEM_BYTES),
    )(*outs)


def solution(mesh):
    sizes = tuple(mesh.shape[a] for a in ("gx", "gy", "gz"))
    return jax.shard_map(
        functools.partial(local, sizes),
        mesh=mesh,
        in_specs=(
            P("gx", "gy", "gz", None),
            P("gx", "gy"),
            P("gx", "gy"),
            P(),
            P(),
            P(),
            P(),
            P("gx", "gy", "gz", None),
        ),
        out_specs=(P("gx", "gy", "gz", None), P("gx", "gy", "gz", None), P(), P(), P()),
        check_vma=False,
    )
```

```python
import functools
import math

import jax
import jax.numpy as jnp
from jax import lax
from jax.experimental import pallas as pl
from jax.experimental.pallas import tpu as pltpu
from jax.sharding import PartitionSpec as P

MESH = pl.DeviceIdType.MESH
F32 = jnp.float32
BF16 = jnp.bfloat16
L = 128
VMEM_BYTES = 63400000
SIDES = [(dx, dy) for dx in (-1, 0, 1) for dy in (-1, 0, 1) if (dx, dy) != (0, 0)]
FACES = [(k, dx, dy) for k in (0, 1) for dx in (-1, 0, 1) for dy in (-1, 0, 1)]


def sigmoid(v):
    return 1.0 / (1.0 + jnp.exp(-v))


def body(
    dims,
    feat_in, ground_in, thick_in, w1_in, w2_in, gains_in, shifts_in, cot_in,
    result_out, gfeat_out, g1_out, g2_out, norm_out,
    feat_ref, cot_ref, w1_ref, w2_ref, gains_ref, shifts_ref, ground_ref, thick_ref,
    result_ref, gfeat_ref, g1_ref, g2_ref, norm_ref,
    HB, S, CT, Y1, Y2, D1, MK, N1, N2, D2,
    ZC, ZY, RC, RX, RY, RK, ZE, MZ, NZ1, NZ2, DZ2,
    V, PS, PH, PD2, PD1, DT, W1, W2, T1, T2, GS,
    STS, RA, RB,
    GA, GC, GF, *rest,
):
    NGX, NGY, NGZ, X, Y, Z, C, segs = dims
    portions = [rest[6 * p : 6 * p + 6] for p in range(3)]
    hs, hr, zs, zr, ss, sr, gs, gr, ins, outs = rest[18:]
    XE, YE = X + 2, Y + 2
    gx, gy, gz = lax.axis_index("gx"), lax.axis_index("gy"), lax.axis_index("gz")
    nz_lo, n_y = NGX // 2, NGZ // 2
    core, z_lo = gx % 2, gx // 2
    row_y, z_hi = gz // 2, gz % 2
    n_z = nz_lo * 2
    pos_z = z_hi * nz_lo + z_lo

    def dev(ax, ay, az):
        return (ax, ay, az)

    def peer_y(j):
        return dev(gx, (gy + j) % NGY, gz)

    def side(dx, dy):
        return dev((gx + dx + NGX) % NGX, (gy + dy + NGY) % NGY, gz)

    def grad_y(j):
        return dev(gx, gy, ((row_y + j) % n_y) * 2 + z_hi)

    def grad_z(j):
        other = (pos_z + j) % n_z
        return dev((other % nz_lo) * 2 + core, gy, row_y * 2 + other // nz_lo)

    partner = dev(z_lo * 2 + 1 - core, gy, gz)
    n_a, n_b = 2 * n_z, NGY * n_y
    me_a, me_b = pos_z * 2 + core, gy * n_y + row_y

    def peer_a(j):
        other = (me_a + j) % n_a
        pos = other // 2
        return dev((pos % nz_lo) * 2 + other % 2, gy, row_y * 2 + pos // nz_lo)

    def peer_b(j):
        other = (me_b + j) % n_b
        return dev(gx, other // n_y, (other % n_y) * 2 + z_hi)

    def beyond(k, dx, dy):
        z = (gz + NGZ - 1) % NGZ if k == 0 else (gz + 1) % NGZ
        return dev((gx + dx + NGX) % NGX, (gy + dy + NGY) % NGY, z)


    greet = [peer_a(j) for j in range(1, n_a)]
    greet += [peer_b(j) for j in range(1, n_b)]
    greet += [beyond(k, dx, dy) for k, dx, dy in FACES]
    greet += [side(dx, dy) for dx, dy in SIDES]
    barrier = pltpu.get_barrier_semaphore()
    for other in greet:
        pl.semaphore_signal(barrier, inc=1, device_id=other, device_id_type=MESH)

    arrivals = [
        pltpu.make_async_copy(src, dst, ins.at[i])
        for i, (src, dst) in enumerate(
            (
                (ground_in, ground_ref), (thick_in, thick_ref), (feat_in, feat_ref),
                (cot_in, cot_ref), (w1_in, w1_ref), (gains_in, gains_ref),
                (shifts_in, shifts_ref), (w2_in, w2_ref),
            )
        )
    ]
    for c in arrivals:
        c.start()

    for ref in (W1, W2, T1, T2, GS):
        ref[...] = jnp.zeros(ref.shape, ref.dtype)
    for c in arrivals[:4]:
        c.wait()

    def load_block(x, carry):
        level = lax.broadcasted_iota(jnp.int32, (Z, L), 0) + gz * Z
        for y in range(Y):
            low = ground_ref[x, y]
            high = low + thick_ref[x, y]
            m = jnp.where((level >= low) & (level < high), 1.0, 0.0).astype(F32)
            S[1 + x, 1 + y] = m
            S[1 + x, 1 + y, :, 0:C] = m[:, 0:C] * feat_ref[x, y].astype(F32)
            CT[1 + x, 1 + y] = jnp.zeros((Z, L), F32)
            CT[1 + x, 1 + y, :, 0:C] = cot_ref[x, y].astype(F32)
            HB[0, 1 + x, 1 + y] = S[1 + x, 1 + y].astype(BF16)
            HB[1, 1 + x, 1 + y] = CT[1 + x, 1 + y].astype(BF16)
        return carry

    lax.fori_loop(0, X, load_block, 0)
    pl.semaphore_wait(barrier, len(greet))

    def cut(d, n, sending):
        if d == 0:
            return pl.ds(1, n)
        if sending:
            return pl.ds(n if d > 0 else 1, 1)
        return pl.ds(0 if d > 0 else n + 1, 1)

    def plane_copies(q):
        out = []
        for k, (dx, dy) in enumerate(SIDES):
            out.append(
                pltpu.make_async_remote_copy(
                    src_ref=HB.at[q, cut(dx, X, True), cut(dy, Y, True)],
                    dst_ref=HB.at[q, cut(dx, X, False), cut(dy, Y, False)],
                    send_sem=hs.at[q, k],
                    recv_sem=hr.at[q, k],
                    device_id=side(dx, dy),
                    device_id_type=MESH,
                )
            )
        return out

    def face_copies(q):
        out = []
        for i, (k, dx, dy) in enumerate(FACES):
            edge_x, side_x = (X - 1, 0) if dx > 0 else (0, 1)
            edge_y, side_y = (1, 0) if dy > 0 else (0, 1)
            if dx and dy:
                src, dst = ZC.at[q, k, edge_x], RK.at[q, 1 - k, side_x, side_y]
            elif dx:
                src, dst = ZC.at[q, k, edge_x], RX.at[q, 1 - k, side_x]
            elif dy:
                src, dst = ZY.at[q, k, edge_y], RY.at[q, 1 - k, side_y]
            else:
                src, dst = ZC.at[q, k], RC.at[q, 1 - k]
            out.append(
                pltpu.make_async_remote_copy(
                    src_ref=src,
                    dst_ref=dst,
                    send_sem=zs.at[int(q == 1), i],
                    recv_sem=zr.at[q, i],
                    device_id=beyond(k, dx, dy),
                    device_id_type=MESH,
                )
            )
        return out

    def start_all(copies):
        for c in copies:
            c.start()

    def wait_all(copies):
        for c in copies:
            c.wait()

    def halo_start(q, ref):
        def one(x, carry):
            for k, z in ((0, 0), (1, Z - 1)):
                ZC[q, k, x] = ref[1 + x, 1 : 1 + Y, z, :].astype(BF16)
            return carry

        start_all(plane_copies(q))
        lax.fori_loop(0, X, one, 0)
        for k, z in ((0, 0), (1, Z - 1)):
            for i, y in ((0, 1), (1, Y)):
                ZY[q, k, i] = ref[1 : 1 + X, y, z, :].astype(BF16)
        start_all(face_copies(q))

    def halo_finish(q, ref):
        wait_all(plane_copies(q))
        wait_all(face_copies(q))
        if q > 1:
            for at in (0, XE - 1):
                ref[at] = HB[q, at].astype(F32)
            for at in (0, YE - 1):
                ref[1 : 1 + X, at] = HB[q, 1 : 1 + X, at].astype(F32)
        for k in range(2):
            def one(x, carry):
                ZE[q, k, 1 + x, 1 : 1 + Y] = RC[q, k, x].astype(F32)
                return carry

            lax.fori_loop(0, X, one, 0)
            for i, at_x in ((0, 0), (1, XE - 1)):
                ZE[q, k, at_x, 1 : 1 + Y] = RX[q, k, i].astype(F32)
                for j, at_y in ((0, 0), (1, YE - 1)):
                    row = Y - 1 if j == 0 else 0
                    tile = RK[q, k, i, j].astype(F32)
                    ZE[q, k, at_x, at_y : at_y + 1] = tile[row : row + 1]
            for j, at_y in ((0, 0), (1, YE - 1)):
                tile = RY[q, k, j].astype(F32)
                for x in range(X):
                    ZE[q, k, 1 + x, at_y : at_y + 1] = tile[x : x + 1]

    def sum_copies(k, part):
        n, me, peer, land = ((n_a, me_a, peer_a, RA), (n_b, me_b, peer_b, RB))[part]
        base = (0, n_a)[part]
        return [
            pltpu.make_async_remote_copy(
                src_ref=STS.at[k, part],
                dst_ref=land.at[k, me],
                send_sem=ss.at[base + j],
                recv_sem=sr.at[k, base + j],
                device_id=peer(j),
                device_id_type=MESH,
            )
            for j in range(1, n)
        ]

    def sum_start(k, part, rows):
        at = lax.broadcasted_iota(jnp.int32, (4, L), 0)
        tile = jnp.zeros((4, L), F32)
        for i, row in enumerate(rows):
            tile = jnp.where(at == i, jnp.broadcast_to(row, (4, L)), tile)
        STS[k, part] = tile
        me, land = ((me_a, RA), (me_b, RB))[part]
        land[k, me] = tile
        start_all(sum_copies(k, part))

    def sum_wait(k, part, spread):
        n, land = ((n_a, RA), (n_b, RB))[part]
        wait_all(sum_copies(k, part))
        tiles = land[k]
        first, second, third = (jnp.sum(tiles[:, i], axis=0, keepdims=True) for i in range(3))
        if not spread:
            return [first, second]
        mean = first / jnp.maximum(third, 1.0)
        each = tiles[:, 0] / jnp.maximum(tiles[:, 2], 1.0) - mean
        second = second + jnp.sum(tiles[:, 2] * each * each, axis=0, keepdims=True)
        return [first, second, third]

    def put(dest, x, main, low, high):
        V[:, 8 : 8 + Z, :] = main
        for y in range(YE):
            V[y, 7:8, :] = low[y : y + 1]
            V[y, 8 + Z : 9 + Z, :] = high[y : y + 1]
        for c in range(3):
            dest[x, :, :, c * L : (c + 1) * L] = V[:, 7 + c : 7 + c + Z, :].astype(BF16)

    H = X // 2

    def convolve(src, weights, flipped, finish):
        def half(h, carry):
            total = None
            for k0 in range(0, 9, 2):
                parts = []
                for k in range(k0, min(k0 + 2, 9)):
                    a, b = k // 3, k % 3
                    if flipped:
                        a, b = 2 - a, 2 - b
                    parts.append(
                        src[pl.ds(h * H + a, H), b : b + Y, :, :].reshape(H * Y * Z, 3 * L)
                    )
                left = jnp.concatenate(parts, axis=1) if len(parts) > 1 else parts[0]
                right = weights[k0 * 3 * L : (k0 * 3 + 3 * len(parts)) * L, :]
                term = jnp.dot(left, right, preferred_element_type=F32)
                total = term if total is None else total + term
            finish(h, total.reshape(H, Y, Z, L))
            return carry

        lax.fori_loop(0, 2, half, 0)

    def own(ref, h):
        return ref[pl.ds(1 + h * H, H), 1 : 1 + Y, :, :]

    def keep(q, ref, h, v):
        ref[pl.ds(1 + h * H, H), 1 : 1 + Y, :, :] = v
        HB[q, pl.ds(1 + h * H, H), 1 : 1 + Y, :, :] = v.astype(BF16)

    def local_sum(terms):
        def one(x, carry):
            return tuple(c + jnp.sum(t, axis=0) for c, t in zip(carry, terms(1 + x)))

        zero = tuple(jnp.zeros((Z, L), F32) for _ in terms(1))
        out = lax.fori_loop(0, X, one, zero)
        return [jnp.sum(v, axis=0, keepdims=True) for v in out]

    def mid(ref, x):
        return ref[x, 1 : 1 + Y, :, :]

    def prepare(get):
        for x in range(X):
            DT[:, x * Y * Z : (x + 1) * Y * Z] = get(1 + x).reshape(Y * Z, L).astype(BF16).T

    def products(g, src, first, last):
        def one(k, carry):
            a, b = k // 3, k % 3
            patch = src[pl.ds(a, X), pl.ds(b, Y), :, :].reshape(X * Y * Z, 3 * L)
            out = jnp.dot(DT[...], patch, preferred_element_type=F32)
            for c in range(3):
                GA[g, pl.ds(pl.multiple_of((3 * k + c) * C, 16), C), :] = (
                    out[:, c * L : (c + 1) * L].T[0:C]
                )
            return carry

        lax.fori_loop(first, last, one, 0, unroll=True)

    axes = ((n_y, row_y, grad_y), (n_z, pos_z, grad_z), (NGY, gy, peer_y))
    plans = []
    base = 0
    for p in range(3):
        plan = [axes[(p + i) % 3] for i in range(3)]
        len1 = plan[1][0] * segs[p]
        plans.append((plan, base, len1, segs[p]))
        base += plan[0][0] * len1
    len_c = base

    def rows_at(off, n):
        return pl.ds(pl.multiple_of(off, 16), n)

    most = max(n_y, n_z, NGY) - 1

    def grad_copies(g, stage):
        def copy(src, dst, k, other):
            return pltpu.make_async_remote_copy(
                src_ref=src, dst_ref=dst, send_sem=gs.at[g, k],
                recv_sem=gr.at[g * 7 + stage if g < 2 else 6 + g * 4 + stage, k], device_id=other, device_id_type=MESH,
            )

        if stage == 0:
            return [copy(GA.at[g, rows_at((1 - core) * len_c, len_c)], GC.at[g], 0, partner)]
        if stage == 6:
            part = GF.at[g, rows_at(core * len_c, len_c)]
            return [copy(part, part, 0, partner)]
        out = []
        for p, (plan, base, len1, seg) in enumerate(plans):
            GB, GY, GD, GZ, GE, GX = portions[p]
            n, me, peer = plan[(None, 0, 1, 2, 1, 0)[stage]]
            off1 = core * len_c + base + plan[0][1] * len1
            off2 = off1 + plan[1][1] * seg
            for j in range(1, n):
                if stage == 1:
                    part = GB.at[g, rows_at(((me + j) % n) * len1, len1)]
                    land = GY.at[g, j - 1]
                elif stage == 2:
                    part = GD.at[g, rows_at(((me + j) % n) * seg, seg)]
                    land = GZ.at[g, j - 1]
                elif stage == 3:
                    part, land = GE.at[g], GX.at[g, me]
                elif stage == 4:
                    part = land = GF.at[g, rows_at(off2, seg)]
                else:
                    part = land = GF.at[g, rows_at(off1, len1)]
                out.append(copy(part, land, p * most + j - 1, peer(j)))
        return out

    def grad_step(g, stage, late=None):
        if stage > 0:
            wait_all(grad_copies(g, stage - 1))
        if stage == 4:
            wait_all(grad_copies(g + 2, 3))
        for p, (plan, base, len1, seg) in enumerate(plans):
            GB, GY, GD, GZ, GE, GX = portions[p]
            if stage == 1:
                def fold(i, carry):
                    at = i * len1 + base
                    GB[g, rows_at(i * len1, len1)] = (
                        GA[g, rows_at(core * len_c + at, len1)] + GC[g, rows_at(at, len1)]
                    )
                    return carry

                lax.fori_loop(0, plan[0][0], fold, 0)
            if stage == 2:
                v = GB[g, rows_at(plan[0][1] * len1, len1)]
                for j in range(plan[0][0] - 1):
                    v = v + GY[g, j]
                GD[g] = v
            if stage == 3:
                v = GD[g, rows_at(plan[1][1] * seg, seg)]
                for j in range(plan[1][0] - 1):
                    v = v + GZ[g, j]
                GE[g] = v
                GX[g, plan[2][1]] = v
            if stage == 4:
                v, w = GX[g, 0], GX[g + 2, 0]
                for j in range(1, plan[2][0]):
                    v = v + GX[g, j]
                    w = w + GX[g + 2, j]
                total, cross, factor = late
                v = factor * (v - (total / count) * spread_lanes(w) - (cross / count) * w)
                off = core * len_c + base + plan[0][1] * len1 + plan[1][1] * seg
                GF[g, rows_at(off, seg)] = v.astype(BF16)
        if stage < 7:
            start_all(grad_copies(g, stage))

    total_cells = X * NGX * Y * NGY * Z * NGZ
    scale = 1.0 / math.sqrt(total_cells / 8.0)

    def grad_store(g, out_ref):
        def one(t, carry):
            out_ref[t] = GF[g, rows_at(t * C, C)].astype(F32)[:, 0:C] * scale
            return carry

        lax.fori_loop(0, 27, one, 0)

    halo_start(0, S)
    for c in arrivals[4:7]:
        c.wait()
    GS[0:2, 0:C] = gains_ref[...]
    GS[2:4, 0:C] = shifts_ref[...]

    def load_first(t, carry):
        W1[pl.ds(pl.multiple_of(t * L, L), C), 0:C] = w1_ref[t]
        return carry

    lax.fori_loop(0, 27, load_first, 0)

    def load_rest(t, carry):
        W2[pl.ds(pl.multiple_of(t * L, L), C), 0:C] = w2_ref[t]
        whole = pl.ds(pl.multiple_of(t * L, L), L)
        back = pl.ds(pl.multiple_of((t - t % 3 + 2 - t % 3) * L, L), L)
        T1[back, :] = W1[whole, :].T
        T2[back, :] = W2[whole, :].T
        return carry

    def fill_weights():
        arrivals[7].wait()
        lax.fori_loop(0, 27, load_rest, 0)

    halo_finish(0, S)
    halo_start(1, CT)

    at_y = lax.broadcasted_iota(jnp.int32, (YE, L), 0)
    live_y = jnp.where(
        ((at_y == 0) & (gy == 0)) | ((at_y == YE - 1) & (gy == NGY - 1)), 0.0, 1.0
    ).astype(F32)
    live_z = [jnp.where(gz == 0, 0.0, 1.0), jnp.where(gz == NGZ - 1, 0.0, 1.0)]

    def spread_lanes(v):
        return jnp.broadcast_to(v[..., L - 1 : L], v.shape)

    def first_input(x, carry):
        gone = ((x == 0) & (gx == 0)) | ((x == XE - 1) & (gx == NGX - 1))
        live = live_y * jnp.where(gone, 0.0, 1.0)
        s = HB[0, x].astype(F32)
        m = spread_lanes(s) * live[:, None, :]
        MK[x] = m
        s = s * m
        S[x] = s
        faces = []
        for k in range(2):
            f = ZE[0, k, x]
            mf = spread_lanes(f) * (live * live_z[k])
            MZ[k, x] = mf
            f = f * mf
            ZE[0, k, x] = f
            faces.append(f)
        put(PS, x, s, faces[0], faces[1])
        return carry

    lax.fori_loop(0, XE, first_input, 0, unroll=2)

    def keep_y1(h, y):
        keep(2, Y1, h, y * own(MK, h))

    convolve(PS, W1, False, keep_y1)

    def norm_begin(k, ref):
        first, count = local_sum(lambda x: (mid(ref, x), mid(MK, x)))
        mean = first / jnp.maximum(count, 1.0)

        def deviation(x):
            d = (mid(ref, x) - mean) * mid(MK, x)
            return (d * d,)

        (second,) = local_sum(deviation)
        return [first, second, count]

    def norm_exchange(k, q, ref, fill):
        rows = norm_begin(k, ref)
        sum_start(k, 0, rows)
        halo_start(q, ref)
        rows = sum_wait(k, 0, True)
        sum_start(k, 1, rows)
        fill()
        halo_finish(q, ref)
        rows = sum_wait(k, 1, True)
        mean = rows[0] / rows[2]
        rstd = lax.rsqrt(rows[1] / rows[2] + 1e-05)
        return mean, rstd, rows[2]

    mean1, rstd1, count = norm_exchange(0, 2, Y1, fill_weights)
    gain1, gain2, shift1, shift2 = GS[0:1], GS[1:2], GS[2:3], GS[3:4]

    def second_input(x, carry):
        def act(y, m):
            n = (y - mean1) * rstd1
            pre = gain1 * n + shift1
            return n, m * (pre * sigmoid(pre))

        n, hidden = act(Y1[x], MK[x])
        N1[x] = n
        faces = []
        for k in range(2):
            nf, hf = act(ZE[2, k, x], MZ[k, x])
            NZ1[k, x] = nf
            faces.append(hf)
        put(PH, x, hidden, faces[0], faces[1])
        return carry

    lax.fori_loop(0, XE, second_input, 0, unroll=2)

    def keep_y2(h, y):
        keep(3, Y2, h, y * own(MK, h))

    convolve(PH, W2, False, keep_y2)
    spare = jnp.where(lax.broadcasted_iota(jnp.int32, (1, L), 1) == L - 1, 1.0, 0.0).astype(F32)

    def second_fill():
        halo_finish(1, CT)
        prepare(lambda x: mid(MK, x) * (mid(N1, x) + spare))
        products(2, PS, 0, 9)
        grad_step(2, 0)

    mean2, rstd2, _ = norm_exchange(1, 3, Y2, second_fill)

    def outgoing(y, s, m, ct):
        n = (y - mean2) * rstd2
        pre = gain2 * n + shift2 + s
        sig = sigmoid(pre)
        return n, m * (pre * sig), ct * m * (sig * (1.0 + pre * (1.0 - sig)))

    lane = lax.broadcasted_iota(jnp.int32, (1, L), 1)
    inner = jnp.where(lane < C, 1.0, 0.0).astype(F32)

    def last_forward(x, carry):
        n, out, d = outgoing(Y2[x], S[x] * inner, MK[x], HB[1, x].astype(F32))
        N2[x] = n
        D2[x] = d

        @pl.when((x >= 1) & (x <= X))
        def _():
            result_ref[x - 1] = out[1 : 1 + Y, :, 0:C].astype(BF16)

        for k in range(2):
            y, s, ct = (ZE[q, k, x] for q in (3, 0, 1))
            nf, _, df = outgoing(y, s * inner, MZ[k, x], ct)
            NZ2[k, x] = nf
            DZ2[k, x] = df
        return carry

    lax.fori_loop(0, XE, last_forward, 0, unroll=2)

    results = [pltpu.make_async_copy(result_ref, result_out, outs.at[0])]
    results[0].start()

    rows = local_sum(lambda x: (mid(D2, x), mid(D2, x) * mid(N2, x)))
    sum_start(2, 0, rows)
    grad_step(2, 1)
    prepare(lambda x: mid(D2, x))
    products(1, PH, 0, 7)
    rows = sum_wait(2, 0, False)
    sum_start(2, 1, rows)
    products(1, PH, 7, 9)
    grad_step(1, 0)
    prepare(lambda x: mid(MK, x) * (mid(N2, x) + spare))
    products(3, PH, 0, 9)
    grad_step(2, 2)
    sum2, cross2 = sum_wait(2, 1, False)
    grad_step(1, 1)
    grad_step(3, 0)

    def third_input(x, carry):
        factor = gain2 * rstd2

        def back(d, n, m):
            return m * factor * (d - sum2 / count - n * cross2 / count)

        main = back(D2[x], N2[x], MK[x])
        faces = [back(DZ2[k, x], NZ2[k, x], MZ[k, x]) for k in range(2)]
        put(PD2, x, main, faces[0], faces[1])
        return carry

    lax.fori_loop(0, XE, third_input, 0, unroll=2)

    def keep_d1(h, v):
        pre = gain1 * own(N1, h) + shift1
        sig = sigmoid(pre)
        keep(4, D1, h, v * own(MK, h) * (sig * (1.0 + pre * (1.0 - sig))))

    convolve(PD2, T2, True, keep_d1)
    rows = local_sum(lambda x: (mid(D1, x), mid(D1, x) * mid(N1, x)))
    sum_start(3, 0, rows)
    halo_start(4, D1)
    grad_step(3, 1)
    prepare(lambda x: mid(D1, x))
    products(0, PS, 0, 9)
    grad_step(0, 0)
    rows = sum_wait(3, 0, False)
    sum_start(3, 1, rows)
    grad_step(1, 2)
    grad_step(2, 3)
    grad_step(0, 1)
    grad_step(3, 2)
    grad_step(1, 3)
    halo_finish(4, D1)
    sum1, cross1 = sum_wait(3, 1, False)

    def fourth_input(x, carry):
        factor = gain1 * rstd1

        def back(d, n, m):
            return m * factor * (d - sum1 / count - n * cross1 / count)

        main = back(D1[x], N1[x], MK[x])
        faces = [back(ZE[4, k, x], NZ1[k, x], MZ[k, x]) for k in range(2)]
        put(PD1, x, main, faces[0], faces[1])
        return carry

    lax.fori_loop(0, XE, fourth_input, 0, unroll=2)

    def keep_features(h, v):
        out = own(MK, h) * (own(D2, h) + v)
        gfeat_ref[pl.ds(h * H, H)] = out[:, :, :, 0:C].astype(BF16)

    convolve(PD1, T1, True, keep_features)
    at8 = lax.broadcasted_iota(jnp.int32, (8, L), 0)
    table = jnp.zeros((8, L), F32)
    for i, row in enumerate((cross1, sum1, cross2, sum2)):
        table = jnp.where(at8 == i, jnp.broadcast_to(row * scale, (8, L)), table)
    norm_ref[...] = table[0:4, 0:C]

    results.append(pltpu.make_async_copy(norm_ref, norm_out, outs.at[1]))
    results.append(pltpu.make_async_copy(gfeat_ref, gfeat_out, outs.at[2]))
    results[1].start()
    results[2].start()

    grad_step(0, 2)
    grad_step(3, 3)
    grad_step(0, 3)
    grad_step(1, 4, (sum2, cross2, gain2 * rstd2))
    grad_step(0, 4, (sum1, cross1, gain1 * rstd1))
    grad_step(1, 5)
    grad_step(0, 5)
    grad_step(1, 6)
    grad_step(0, 6)
    grad_step(1, 7)
    grad_store(1, g2_ref)
    results.append(pltpu.make_async_copy(g2_ref, g2_out, outs.at[3]))
    results[3].start()
    grad_step(0, 7)
    grad_store(0, g1_ref)
    results.append(pltpu.make_async_copy(g1_ref, g1_out, outs.at[4]))
    results[4].start()
    for c in results:
        c.wait()


def hand_over(*refs):
    ins, outs, held, (into, out) = refs[0:5], refs[5:10], refs[10:15], refs[15:17]
    first = [pltpu.make_async_copy(a, b, into.at[i]) for i, (a, b) in enumerate(zip(ins, held))]
    last = [pltpu.make_async_copy(a, b, out.at[i]) for i, (a, b) in enumerate(zip(held, outs))]
    for c in first:
        c.start()
    for a, b in zip(first, last):
        a.wait()
        b.start()
    for c in last:
        c.wait()


def local(sizes, features, ground, thickness, weight_one, weight_two, gains, shifts, cotangent):
    NGX, NGY, NGZ = sizes
    X, Y, Z, C = features.shape
    n_y, n_z = NGZ // 2, NGX
    n = (n_y, n_z, NGY)
    pairs = [n[p] * n[(p + 1) % 3] for p in range(3)]
    tiles = -(-27 * C // (2 * 16 * min(pairs)))
    segs = tuple(16 * (tiles // 3 + (p < tiles % 3)) for p in range(3))
    dims = (NGX, NGY, NGZ, X, Y, Z, C, segs)
    XE, YE = X + 2, Y + 2
    ext = pltpu.VMEM((XE, YE, Z, L), F32)
    face = pltpu.VMEM((2, XE, YE, L), F32)
    patch = pltpu.VMEM((XE, YE, Z, 3 * L), BF16)
    weights = pltpu.VMEM((27 * L, L), BF16)
    dma = pltpu.SemaphoreType.DMA
    scratch = [
        pltpu.VMEM((X, Y, Z, C), BF16),
        pltpu.VMEM((X, Y, Z, C), BF16),
        pltpu.VMEM((27, C, C), BF16),
        pltpu.VMEM((27, C, C), BF16),
        pltpu.VMEM((2, C), F32),
        pltpu.VMEM((2, C), F32),
        pltpu.SMEM((X, Y), jnp.int32),
        pltpu.SMEM((X, Y), jnp.int32),
        pltpu.VMEM((X, Y, Z, C), BF16),
        pltpu.VMEM((X, Y, Z, C), BF16),
        pltpu.VMEM((27, C, C), F32),
        pltpu.VMEM((27, C, C), F32),
        pltpu.VMEM((4, C), F32),
    ]
    scratch += [pltpu.VMEM((5, XE, YE, Z, L), BF16)]
    scratch += [ext] * 9
    scratch += [
        pltpu.VMEM((5, 2, X, Y, L), BF16),
        pltpu.VMEM((5, 2, 2, X, L), BF16),
        pltpu.VMEM((5, 2, X, Y, L), BF16),
        pltpu.VMEM((5, 2, 2, Y, L), BF16),
        pltpu.VMEM((5, 2, 2, X, L), BF16),
        pltpu.VMEM((5, 2, 2, 2, Y, L), BF16),
        pltpu.VMEM((5, 2, XE, YE, L), F32),
    ]
    scratch += [face] * 4
    scratch += [pltpu.VMEM((YE, Z + 16, L), F32)]
    scratch += [patch] * 4
    scratch += [pltpu.VMEM((L, X * Y * Z), BF16)]
    scratch += [weights] * 4
    scratch += [pltpu.VMEM((8, L), F32)]
    n_a, n_b = 2 * n_z, NGY * n_y
    scratch += [pltpu.VMEM((4, 2, 4, L), F32)]
    scratch += [pltpu.VMEM((4, k, 4, L), F32) for k in (n_a, n_b)]
    len_c = sum(a * b for a, b in zip(pairs, segs))
    scratch += [
        pltpu.VMEM((4, 2 * len_c, L), F32),
        pltpu.VMEM((4, len_c, L), F32),
        pltpu.VMEM((2, 2 * len_c, L), BF16),
    ]
    for p in range(3):
        n1, n2, n3 = n[p], n[(p + 1) % 3], n[(p + 2) % 3]
        seg = segs[p]
        scratch += [
            pltpu.VMEM((4, n1 * n2 * seg, L), F32),
            pltpu.VMEM((4, n1 - 1, n2 * seg, L), F32),
            pltpu.VMEM((4, n2 * seg, L), F32),
            pltpu.VMEM((4, n2 - 1, seg, L), F32),
            pltpu.VMEM((4, seg, L), F32),
            pltpu.VMEM((4, n3, seg, L), F32),
        ]
    most = max(n) - 1
    scratch += [dma((5, 8)), dma((5, 8)), dma((2, 18)), dma((5, 18))]
    scratch += [dma((n_a + n_b,)), dma((4, n_a + n_b))]
    scratch += [dma((4, 3 * most)), dma((22, 3 * most))]
    scratch += [dma((8,)), dma((5,))]
    anywhere = pl.BlockSpec(memory_space=pl.ANY)
    shapes = (
        jax.ShapeDtypeStruct((X, Y, Z, C), BF16),
        jax.ShapeDtypeStruct((X, Y, Z, C), BF16),
        jax.ShapeDtypeStruct((27, C, C), F32),
        jax.ShapeDtypeStruct((27, C, C), F32),
        jax.ShapeDtypeStruct((4, C), F32),
    )
    outs = pl.pallas_call(
        functools.partial(body, dims),
        out_shape=shapes,
        in_specs=[pl.BlockSpec(memory_space=pltpu.HBM)] * 8,
        out_specs=(anywhere,) * 5,
        scratch_shapes=scratch,
        compiler_params=pltpu.CompilerParams(
            collective_id=0, has_side_effects=True, vmem_limit_bytes=VMEM_BYTES
        ),
    )(features, ground, thickness, weight_one, weight_two, gains, shifts, cotangent)
    return pl.pallas_call(
        hand_over,
        out_shape=shapes,
        in_specs=[anywhere] * 5,
        out_specs=(pl.BlockSpec(memory_space=pltpu.HBM),) * 5,
        scratch_shapes=[pltpu.VMEM(v.shape, v.dtype) for v in shapes] + [dma((5,)), dma((5,))],
        compiler_params=pltpu.CompilerParams(vmem_limit_bytes=VMEM_BYTES),
    )(*outs)


def solution(mesh):
    sizes = tuple(mesh.shape[a] for a in ("gx", "gy", "gz"))
    return jax.shard_map(
        functools.partial(local, sizes),
        mesh=mesh,
        in_specs=(
            P("gx", "gy", "gz", None),
            P("gx", "gy"),
            P("gx", "gy"),
            P(),
            P(),
            P(),
            P(),
            P("gx", "gy", "gz", None),
        ),
        out_specs=(P("gx", "gy", "gz", None), P("gx", "gy", "gz", None), P(), P(), P()),
        check_vma=False,
    )
```
